32 devices in a mesh: seq: 8 (over z, y), view: 4 (over x, core).
Axes of the slice: x: 2, y: 2, z: 4, core: 2. Of those that a mesh axis runs over, the one named last changes fastest.
Arguments:
- ssd_input: bfloat16 [8, 4, 512, 2048], P('seq', 'view'), may hold values from -21 to 21
- gate_input: bfloat16 [8, 4, 512, 2048], P('seq', 'view'), may hold values from -6 to 6
- b_matrix: bfloat16 [8, 4, 512, 128], P('seq', 'view'), may hold values from -6 to 6
- c_matrix: bfloat16 [8, 4, 512, 128], P('seq', 'view'), may hold values from -0.52734375 to 0.52734375
- log_decay: float32 [8, 4, 32, 512], P('seq', 'view'), may hold values from -1 to 0, as said below
- d_skip: float32 [32], replicated, may hold values from 1 to 4
- norm_gain: float32 [2048], replicated, may hold values from 0.1 to 1.9
- out_weight: bfloat16 [2048, 1536], replicated, may hold values from -0.125 to 0.125
- view_order: int32 [8, 4], P('seq'), may hold values from 0 to 3, each once within a row
- tile_order: int32 [8, 4], P('seq'), may hold values from 0 to 3, each once within a row
Outputs:
- next_tokens: bfloat16 [8, 4, 512, 1536], P('seq', 'view')
The draws below stay inside these ranges and needn't reach their ends.
Inputs may be any that keep to these rules, and one draw needn't show every extreme that they name: `log_decay`: negative everywhere. `view_order`: each row is a permutation of the views. `tile_order`: each row is a permutation of the tiles of a block.
All inputs are finite; a program needn't handle non-finite values.
Results may differ from the reference program's by a relative error of at most 0.0059.
Values may be sent and summed in bfloat16 or wider, within the bound.
A program may use at most 128 MiB of HBM per device.

```python
import jax
import jax.numpy as jnp
from jax import lax

H = 32
HEAD = 64
N = 128
D_OUT = 1536
GROUP = 256
TILE = 128
TOKENS_PER_BLOCK = 512
DI = 2048
BAND_TOTAL = 8
VIEW_TOTAL = 4
PIECE = 64
TILES_DEV = 4


def draw_ssd_input(key, part):
    random_subkeys = jax.random.split(key, 3)
    channel_scale = jnp.exp(jax.random.uniform(random_subkeys[0], (H * HEAD,), jnp.float32, jnp.log(0.3), jnp.log(3.0)))
    token_scale = jnp.exp(jax.random.uniform(random_subkeys[1], (BAND_TOTAL, VIEW_TOTAL, TOKENS_PER_BLOCK, 1), jnp.float32, jnp.log(0.6), jnp.log(1.7)))
    values = jnp.clip(jax.random.normal(random_subkeys[2], (BAND_TOTAL, VIEW_TOTAL, TOKENS_PER_BLOCK, H * HEAD), jnp.float32), -4.0, 4.0)
    return (values * token_scale * channel_scale).astype(jnp.bfloat16)


def draw_log_decay(key, part):
    random_subkeys = jax.random.split(key, 7)
    sequence_length = BAND_TOTAL * VIEW_TOTAL * TOKENS_PER_BLOCK
    fast_share = 0.5
    fast_heads = jax.random.uniform(random_subkeys[0], (H,), jnp.float32) < fast_share
    slow_rate = jnp.exp(jax.random.uniform(random_subkeys[1], (H,), jnp.float32, jnp.log(0.1), jnp.log(0.5))) / sequence_length
    fast_rate = jnp.exp(jax.random.uniform(random_subkeys[2], (H,), jnp.float32, jnp.log(1.0 / 60.0), jnp.log(1.0 / 25.0)))
    head_decay_rate = jnp.where(fast_heads, fast_rate, slow_rate)
    block_multiplier = jnp.exp(jax.random.uniform(random_subkeys[3], (BAND_TOTAL, VIEW_TOTAL, 1, 1), jnp.float32, jnp.log(0.5), jnp.log(2.0)))
    token_multiplier = jnp.exp(jax.random.uniform(random_subkeys[4], (BAND_TOTAL, VIEW_TOTAL, H, TOKENS_PER_BLOCK), jnp.float32, jnp.log(0.5), jnp.log(2.0)))
    spike_positions = jax.random.randint(random_subkeys[5], (3,), 0, sequence_length)
    spike_keep_mask = jnp.log(jax.random.uniform(random_subkeys[6], (3,), jnp.float32, 0.6, 0.8))
    token_positions = jnp.arange(sequence_length, dtype=jnp.int32).reshape(BAND_TOTAL, VIEW_TOTAL, 1, TOKENS_PER_BLOCK)
    spike_log_decay = jnp.zeros((BAND_TOTAL, VIEW_TOTAL, 1, TOKENS_PER_BLOCK), jnp.float32)
    for lookup_index in range(3):
        spike_log_decay = spike_log_decay + jnp.where(token_positions == spike_positions[lookup_index], spike_keep_mask[lookup_index], 0.0)
    return -head_decay_rate[None, None, :, None] * block_multiplier * token_multiplier + spike_log_decay


def block_scale(rng, shape, shards, smallest, top_value):
    def one(axis_at, shards_of):
        steps = jax.random.uniform(jax.random.fold_in(jax.random.fold_in(rng, 6), axis_at), (shards_of,), jnp.float32, smallest / len(shards), top_value / len(shards))
        return jnp.repeat(jnp.exp(steps), shape[axis_at] // shards_of).reshape((-1,) + (1,) * (len(shape) - axis_at - 1))

    gain = one(*shards[0])
    for cut in shards[1:]:
        gain = gain * one(*cut)
    return gain


def normal_values(stream_key, dims, deviation, bound, shards=(), held_as=jnp.bfloat16):
    drawn = deviation * jax.random.normal(stream_key, dims, jnp.float32)
    if shards:
        drawn = drawn * block_scale(stream_key, dims, shards, -0.22, 0.18)
    return jnp.clip(drawn, -bound, bound).astype(held_as)


def setup_inputs(seed: int = 0) -> dict:
    key_list = jax.random.split(jax.random.key(seed), 11)
    return {
        "ssd_input": draw_ssd_input(jax.random.fold_in(key_list[10], 71), 0),
        "gate_input": normal_values(key_list[1], (BAND_TOTAL, VIEW_TOTAL, TOKENS_PER_BLOCK, DI), 1.0, 6.0, ((0, 8), (1, 4))),
        "b_matrix": normal_values(key_list[2], (BAND_TOTAL, VIEW_TOTAL, TOKENS_PER_BLOCK, N), 1.0, 6.0, ((0, 8), (1, 4))),
        "c_matrix": normal_values(key_list[3], (BAND_TOTAL, VIEW_TOTAL, TOKENS_PER_BLOCK, N), 0.088, 0.52734375, ((0, 8), (1, 4))),
        "log_decay": draw_log_decay(jax.random.fold_in(key_list[10], 71), 0),
        "d_skip": jnp.clip(jax.random.uniform(key_list[5], (H,), jnp.float32, 1.0, 4.0), 1.0, 4.0),
        "norm_gain": jnp.clip(1.0 + 0.18 * jax.random.normal(key_list[6], (DI,), jnp.float32), 0.1, 1.9),
        "out_weight": normal_values(key_list[7], (DI, D_OUT), DI ** -0.5, 0.125),
        "view_order": jax.vmap(lambda own: jax.random.permutation(own, VIEW_TOTAL))(jax.random.split(key_list[8], BAND_TOTAL)).reshape((BAND_TOTAL, VIEW_TOTAL)).astype(jnp.int32),
        "tile_order": jax.vmap(lambda own: jax.random.permutation(own, TILES_DEV))(jax.random.split(key_list[9], BAND_TOTAL)).reshape((BAND_TOTAL, TILES_DEV)).astype(jnp.int32),
    }


EPS = 1e-05

def group_parts(x_block, b_block, c_block, g_block):
    group_count = TOKENS_PER_BLOCK // GROUP
    cum_log = jnp.cumsum(g_block.reshape(H, group_count, GROUP), axis=2)
    group_end = cum_log[:, :, GROUP - 1]
    x_groups = x_block.reshape(group_count, GROUP, H, HEAD).astype(jnp.float32)
    b_groups = b_block.reshape(group_count, GROUP, N).astype(jnp.float32)
    c_groups = c_block.reshape(group_count, GROUP, N).astype(jnp.float32)
    return (cum_log, group_end, x_groups, b_groups, c_groups)

def group_states(cum_log, group_end, x_groups, b_groups):
    scaled = jnp.exp(group_end[:, :, None] - cum_log)[..., None] * b_groups[None]
    scaled = lax.optimization_barrier(scaled.astype(jnp.bfloat16)).astype(jnp.float32)
    return jnp.einsum('hckn,ckhp->hcpn', scaled, x_groups)

def summary(block):
    x_block, b_block, c_block, g_block = block
    cum_log, group_end, x_groups, b_groups, c_groups = group_parts(x_block, b_block, c_block, g_block)
    states = group_states(cum_log, group_end, x_groups, b_groups)
    group_decay = jnp.exp(group_end)
    total = jnp.ones((H,), jnp.float32)
    running = jnp.zeros((H, HEAD, N), jnp.float32)
    for lookup_index in range(TOKENS_PER_BLOCK // GROUP):
        running = group_decay[:, lookup_index, None, None] * running + states[:, lookup_index]
        total = total * group_decay[:, lookup_index]
    return (total, running)

def reference(ssd_input, gate_input, b_matrix, c_matrix, log_decay, d_skip, norm_gain, out_weight, view_order, tile_order):
    group_count = TOKENS_PER_BLOCK // GROUP
    blocks = BAND_TOTAL * VIEW_TOTAL
    x_all = ssd_input.reshape(blocks, TOKENS_PER_BLOCK, H * HEAD)
    z_all = gate_input.reshape(blocks, TOKENS_PER_BLOCK, H * HEAD)
    b_all = b_matrix.reshape(blocks, TOKENS_PER_BLOCK, N)
    c_all = c_matrix.reshape(blocks, TOKENS_PER_BLOCK, N)
    g_all = log_decay.reshape(blocks, H, TOKENS_PER_BLOCK)
    totals, states = lax.map(summary, (x_all, b_all, c_all, g_all))
    totals = totals.reshape(BAND_TOTAL, VIEW_TOTAL, H)
    states = states.reshape(BAND_TOTAL, VIEW_TOTAL, H, HEAD, N)

    def row_step(carry, row):
        row_totals, row_states, row_order = row
        entering = jnp.zeros((VIEW_TOTAL, H, HEAD, N), jnp.float32)
        for rank_pos in range(VIEW_TOTAL):
            view_now = row_order[rank_pos]
            entering = entering.at[view_now].set(carry)
            carry = jnp.take(row_totals, view_now, axis=0)[:, None, None] * carry + jnp.take(row_states, view_now, axis=0)
        return (carry, entering)
    _, entering = lax.scan(row_step, jnp.zeros((H, HEAD, N), jnp.float32), (totals, states, view_order))
    entering = entering.reshape(blocks, H, HEAD, N)
    causal = jnp.tril(jnp.ones((GROUP, GROUP), dtype=bool))

    def block_out(block):
        x_block, z_block, b_block, c_block, g_block, start = block
        cum_log, group_end, x_groups, b_groups, c_groups = group_parts(x_block, b_block, c_block, g_block)
        states_here = group_states(cum_log, group_end, x_groups, b_groups)
        group_decay = jnp.exp(group_end)
        scores = jnp.einsum('cqn,ckn->cqk', c_groups, b_groups)
        log_gaps = cum_log[:, :, :, None] - cum_log[:, :, None, :]
        weights = jnp.exp(jnp.where(causal, log_gaps, -jnp.inf)) * scores[None]
        weights = lax.optimization_barrier(weights.astype(jnp.bfloat16)).astype(jnp.float32)
        inside = jnp.einsum('hcqk,ckhp->cqhp', weights, x_groups)
        running = start
        collected = []
        for lookup_index in range(group_count):
            collected.append(running)
            running = group_decay[:, lookup_index, None, None] * running + states_here[:, lookup_index]
        entry = jnp.stack(collected, axis=1)
        entry = lax.optimization_barrier(entry.astype(jnp.bfloat16)).astype(jnp.float32)
        carried = jnp.einsum('cqn,hcpn->cqhp', c_groups, entry) * jnp.transpose(jnp.exp(cum_log), (1, 2, 0))[..., None]
        mixed = inside + carried + d_skip[None, None, :, None] * x_groups
        gate_vals = z_block.reshape(group_count, GROUP, H, HEAD).astype(jnp.float32)
        gated = mixed * jax.nn.silu(gate_vals)
        inv_rms = lax.rsqrt(lax.optimization_barrier(jnp.mean(gated * gated, axis=-1, keepdims=True)) + EPS)
        normed = (gated * inv_rms * norm_gain.reshape(H, HEAD)).astype(jnp.bfloat16).reshape(TOKENS_PER_BLOCK, H * HEAD)
        return jnp.dot(normed, out_weight, preferred_element_type=jnp.float32).astype(jnp.bfloat16)
    projected = lax.map(block_out, (x_all, z_all, b_all, c_all, g_all, entering))
    projected = projected.reshape(BAND_TOTAL, VIEW_TOTAL, BAND_TOTAL, PIECE, D_OUT)
    reordered = jnp.transpose(projected, (2, 1, 0, 3, 4)).reshape(BAND_TOTAL, VIEW_TOTAL, TILES_DEV, TILE, D_OUT)
    picked = jax.vmap(lambda band_rows, order_row: jnp.take(band_rows, order_row, axis=1))(reordered, tile_order)
    return picked.reshape(BAND_TOTAL, VIEW_TOTAL, TOKENS_PER_BLOCK, D_OUT)
```

```python
import functools
import math

import jax
import jax.numpy as jnp
from jax import lax
from jax.experimental import pallas as pl
from jax.experimental.pallas import tpu as pltpu
from jax.sharding import PartitionSpec as P

GROUP = 256
TILE = 128
EPS = 1e-05
LOG2E = math.log2(math.e)
MESH = pl.DeviceIdType.MESH
F32 = jnp.float32
BF16 = jnp.bfloat16
VMEM = pltpu.VMEM
VMEM_LIMIT = 48 * 1000 * 1000


def nn(a, b):
    return lax.dot_general(a, b, (((1,), (0,)), ((), ())), preferred_element_type=F32)


def nt(a, b):
    return lax.dot_general(a, b, (((1,), (1,)), ((), ())), preferred_element_type=F32)


def split2(a):
    hi = a.astype(BF16)
    return hi, (a - hi.astype(F32)).astype(BF16)


def split3(a):
    hi = a.astype(BF16)
    rest = a - hi.astype(F32)
    mid = rest.astype(BF16)
    low = (rest - mid.astype(F32)).astype(BF16)
    return hi, mid, low


def iota(shape, dim):
    return lax.broadcasted_iota(jnp.int32, shape, dim)


def pair_columns(full, pair):
    lanes = full.shape[1]
    turned = pltpu.roll(full, lax.rem(lanes - 2 * pair, lanes), 1)
    return turned[:, 0:1], turned[:, 1:2]


def spread(first, width):
    row = iota((256, width), 0)
    head = jnp.where(row < 128, row, row - 128)
    return jnp.where(head == first + (iota((256, width), 1) >> 6), 1.0, 0.0).astype(BF16)


def mixer_kernel(
    views, pack, groups, batches, bands,
    order_ref, skip_ref, b_ref, c_ref, ld_ref, gain_ref, x_hbm, gate_hbm, w_hbm,
    out_hbm,
    x_s, gate_s, w_s, p_s, q_s, sem_x, sem_g, sem_w, sem_o,
    col_ref, row_ref, score_ref, bt_s, scale2_s, ecol2_s, dec_s, total_s, prefix_s,
    note_s, gotnote_s, aggnote_s, aggnotes_s, coef_s, before_s, last_s,
    state_s, got_s, agg_s, aggs_s, within_s, carry_s, send_s, ent_s,
    sem_n, sem_a, sem_bn, sem_b, sem_c,
    entry_s, normed_s, mine_s, sem,
):
    band, view = lax.axis_index("seq"), lax.axis_index("view")
    count = views * pack
    chips = count // 2
    group, member = band // pack, lax.rem(band, pack)
    me = member * views + view
    heads, tokens = ld_ref.shape
    spans = tokens // GROUP
    width = x_s.shape[1]
    pairs = width // 128
    HALF = GROUP // 2

    load = pltpu.make_async_copy(x_hbm, x_s, sem_x)
    load_gate = pltpu.make_async_copy(gate_hbm, gate_s, sem_g)
    load_w = pltpu.make_async_copy(w_hbm, w_s, sem_w)
    load.start()
    load_gate.start()
    load_w.start()

    barrier = pltpu.get_barrier_semaphore()
    for d in range(1, bands):
        pl.semaphore_signal(
            barrier, inc=1,
            device_id={"seq": lax.rem(band + d, bands), "view": view}, device_id_type=MESH,
        )
    for d in range(1, views):
        for m in range(pack):
            pl.semaphore_signal(
                barrier, inc=1,
                device_id={"seq": group * pack + m, "view": lax.rem(view + d, views)},
                device_id_type=MESH,
            )

    at_row, at_col = iota((GROUP, GROUP), 0), iota((GROUP, GROUP), 1)
    lower = jnp.where(at_col <= at_row, 1.0, 0.0).astype(BF16)
    upper = jnp.where(at_row <= at_col, 1.0, 0.0).astype(BF16)
    total = jnp.zeros((heads, 1), F32)
    for c in range(spans):
        span = slice(c * GROUP, (c + 1) * GROUP)
        own = ld_ref[:, span] * LOG2E
        padded = jnp.concatenate([own, jnp.zeros((128 - heads, GROUP), F32)], axis=0)
        lines = sum(nn(part, upper) for part in split3(own))
        row_ref[:, span] = lines
        cols = sum(nt(lower, part) for part in split3(padded))
        col_ref[span, :] = cols
        for ref, value in (
            (ecol2_s, jnp.exp2(cols)),
            (scale2_s, jnp.exp2(jnp.minimum(cols[GROUP - 1 : GROUP, :] - cols, 0.0))),
        ):
            hi, lo = split2(value)
            ref[span, 0:128] = hi
            ref[span, 128:256] = lo
        total = total + lines[:, GROUP - 1 : GROUP]
        bt_s[:, span] = b_ref[span, :].astype(F32).T.astype(BF16)
    total_s[...] = jnp.broadcast_to(total, total_s.shape)

    rank = jnp.int32(0)
    for r in range(views):
        rank = rank + jnp.where(order_ref[0, r] == view, r, 0)
    key = (rank + member * views).astype(F32)
    left = iota((1, 128), 1) < 64
    for q in range(count):
        for j in range(batches):
            head = 2 * (j * count + q)
            note_s[q, j : j + 1, :] = jnp.where(
                left, total_s[head : head + 1, :], total_s[head + 1 : head + 2, :]
            )
        note_s[q, batches : batches + 1, :] = jnp.full((1, 128), key, F32)

    def peer(q):
        return {"seq": group * pack + q // views, "view": lax.rem(q, views)}

    def exchange(source, target, sends, receives, q):
        return pltpu.make_async_remote_copy(
            src_ref=source, dst_ref=target, send_sem=sends, recv_sem=receives,
            device_id=peer(q), device_id_type=MESH,
        )

    def note_copy(q, slot):
        return exchange(note_s.at[q], gotnote_s.at[slot], sem_n.at[0, q], sem_n.at[1, slot], q)

    def state_copy(j, q, slot):
        return exchange(
            state_s.at[j, q], got_s.at[j, slot], sem_a.at[j, 0, q], sem_a.at[j, 1, slot], q
        )

    def enter_copy(j, q, slot):
        return exchange(
            send_s.at[j, q], ent_s.at[j, slot], sem_c.at[j, 0, q], sem_c.at[j, 1, slot], q
        )

    def others():
        return [lax.rem(me + d, count) for d in range(1, count)]

    def ahead(source, target, sems, k, g):
        return pltpu.make_async_remote_copy(
            src_ref=source, dst_ref=target, send_sem=sems.at[0, k], recv_sem=sems.at[1, k],
            device_id={"seq": g * pack + member, "view": view}, device_id_type=MESH,
        )

    def aggnote_copy(k, g):
        return ahead(aggnote_s, aggnotes_s.at[k], sem_bn, k, g)

    def agg_copy(j, k, g):
        return ahead(agg_s.at[j], aggs_s.at[j, k], sem_b.at[j], k, g)

    def later(run):
        for k in range(groups - 1, 0, -1):
            @pl.when(group + k < groups)
            def _(k=k):
                run(k, group + k)

    def earlier(run):
        for k in range(groups - 1, 0, -1):
            @pl.when(group - k >= 0)
            def _(k=k):
                run(k, group - k)

    pl.semaphore_wait(barrier, bands - 1 + (views - 1) * pack)
    for q in others():
        note_copy(q, me).start()

    def states(j, chip):
        base = j * count + 2 * chip
        lanes = pl.ds(pl.multiple_of(base * 128, 256), 256)
        pick = spread(2 * base, 256)
        running = jnp.zeros((128, 256), F32)
        for c in range(spans):
            span = slice(c * GROUP, (c + 1) * GROUP)
            scale = nn(scale2_s[span, :], pick)
            made = nn(bt_s[:, span], (x_s[span, lanes].astype(F32) * scale).astype(BF16))
            ends = nn(ecol2_s[(c + 1) * GROUP - 16 : (c + 1) * GROUP, :], pick)
            dec = ends[15:16, :]
            prefix_s[c, :, lanes] = running
            dec_s[c, :, lanes] = jnp.broadcast_to(dec, (8, 256))
            running = dec * running + made if c else made
        for i in range(2):
            state_s[j, 2 * chip + i] = running[:, i * 128 : (i + 1) * 128].astype(BF16)

    mychip = me // 2
    partner = me + 1 - 2 * lax.rem(me, 2)
    load.wait()
    for j in range(batches):
        for d in range(1, chips):
            chip = lax.rem(mychip + d, chips)
            states(j, chip)
            for i in range(2):
                state_copy(j, 2 * chip + i, me).start()
        states(j, mychip)
        state_copy(j, partner, me).start()
        got_s[j, me] = state_s[j, me]

    for c in range(spans):
        span = slice(c * GROUP, (c + 1) * GROUP)
        scores = nt(c_ref[span, :], b_ref[span, :])
        score_ref[c] = jnp.where(at_col <= at_row, scores, 0.0)

    first_half = iota((GROUP, 128), 1) < 64

    def inside_span(start, stop):
        @pl.loop(start, stop)
        def _(pair):
            cols = pair_columns(col_ref[...], pair)
            lanes = pl.ds(pl.multiple_of(pair * 128, 128), 128)
            pick = spread(2 * pair, 128)
            for c in range(spans):
                span = slice(c * GROUP, (c + 1) * GROUP)
                x = x_s[span, lanes]
                outs = []
                for j, col in enumerate(cols):
                    line = row_ref[pl.ds(2 * pair + j, 1), span]
                    col = col[span, :]
                    top = jnp.minimum(col[:HALF] - line[:, :HALF], 0.0)
                    top = (jnp.exp2(top) * score_ref[c, :HALF, :HALF]).astype(BF16)
                    low = jnp.minimum(col[HALF:] - line, 0.0)
                    low = (jnp.exp2(low) * score_ref[c, HALF:, :]).astype(BF16)
                    outs.append(jnp.concatenate([nn(top, x[:HALF]), nn(low, x)], axis=0))
                gate = gate_s[span, lanes].astype(F32)
                silu = gate / (1.0 + jnp.exp(-gate))
                q_s[span, lanes] = nn(ecol2_s[span, :], pick) * silu
                made = jnp.where(first_half, outs[0], outs[1]) + jnp.where(
                    first_half, skip_ref[2 * pair], skip_ref[2 * pair + 1]
                ) * x.astype(F32)
                p_s[span, lanes] = made * silu

    cuts = CUTS(pairs)
    load_gate.wait()
    inside_span(cuts[0], cuts[1])

    gotnote_s[me] = note_s[me]
    for q in others():
        note_copy(q, q).wait_recv()
    logs = [gotnote_s[b] for b in range(count)]
    keys = [jnp.broadcast_to(log[batches : batches + 1, :], log.shape) for log in logs]
    zero = jnp.zeros_like(logs[0])
    upto, whole = [], zero
    for b in range(count):
        acc = zero
        for o in range(count):
            if o != b:
                acc = acc + jnp.where(keys[o] < keys[b], logs[o], 0.0)
        upto.append(acc + logs[b])
        before_s[b] = jnp.exp2(acc)
        for o in range(count):
            coef_s[b, o] = acc
        whole = whole + logs[b]
    aggnote_s[...] = whole
    later(lambda k, g: aggnote_copy(k, g).start())
    for b in range(count):
        last_s[b] = jnp.exp2(jnp.minimum(whole - upto[b], 0.0))
        for o in range(count):
            if o != b:
                coef_s[b, o] = jnp.where(
                    keys[o] < keys[b], jnp.exp2(jnp.minimum(coef_s[b, o] - upto[o], 0.0)), 0.0
                )

    for j in range(batches):
        for q in others():
            state_copy(j, q, q).wait_recv()
        for i in range(4):
            part = slice(i * 32, (i + 1) * 32)
            acc = jnp.zeros((32, 128), F32)
            for b in range(count):
                acc = acc + last_s[b, j : j + 1, :] * got_s[j, b, part, :].astype(F32)
            agg_s[j, part, :] = acc.astype(BF16)
        later(lambda k, g: agg_copy(j, k, g).start())
        for i in range(4):
            part = slice(i * 32, (i + 1) * 32)
            blocks = [got_s[j, o, part, :].astype(F32) for o in range(count)]
            for b in range(count):
                acc = jnp.zeros((32, 128), F32)
                for o in range(count):
                    if o != b:
                        acc = acc + coef_s[b, o, j : j + 1, :] * blocks[o]
                within_s[j, b, part, :] = acc

    inside_span(cuts[1], cuts[2])

    earlier(lambda k, g: aggnote_copy(k, g).wait_recv())
    for j in range(batches):
        carry_s[...] = jnp.zeros_like(carry_s)

        def gather(k, g):
            agg_copy(j, k, g).wait_recv()
            decay = jnp.exp2(aggnotes_s[k, j : j + 1, :])
            carry_s[...] = decay * carry_s[...] + aggs_s[j, k].astype(F32)

        earlier(gather)

        def entering(q):
            return (before_s[q, j : j + 1, :] * carry_s[...] + within_s[j, q]).astype(BF16)

        for q in others():
            send_s[j, q] = entering(q)
            enter_copy(j, q, me).start()
        ent_s[j, me] = entering(me)

    inside_span(cuts[2], cuts[3])

    piece = mine_s.shape[1]
    width_out = w_s.shape[1]
    chunk = normed_s.shape[0]
    chunks = tokens // chunk
    half = chunks // 2
    per_chunk = chunk // piece
    turn = lax.rem(band // per_chunk, half)
    mine_half = band // (bands // 2)
    same = (iota((256, 256), 0) >> 6) == (iota((256, 256), 1) >> 6)
    block = jnp.where(same, 1.0 / 64.0, 0.0).astype(BF16)
    quads = width // 256

    def send(j):
        return pltpu.make_async_remote_copy(
            src_ref=mine_s.at[j], dst_ref=out_hbm.at[band],
            send_sem=sem.at[0, j], recv_sem=sem.at[1, band],
            device_id={"seq": j, "view": view}, device_id_type=MESH,
        )

    def arrival(i):
        return pltpu.make_async_remote_copy(
            src_ref=mine_s.at[i], dst_ref=out_hbm.at[i],
            send_sem=sem.at[0, i], recv_sem=sem.at[1, i],
            device_id={"seq": i, "view": view}, device_id_type=MESH,
        )

    def entry_of(c, j):
        for q in range(count):
            at = (j * count + q) * 128
            lanes = slice(at, at + 128)
            made = ent_s[j, q].astype(F32)
            entry_s[:, lanes] = (before_of(c, lanes) * made + prefix_s[c, :, lanes]).astype(BF16)

    def before_of(c, lanes):
        made = jnp.ones((1, lanes.stop - lanes.start), F32)
        for o in range(spans - 1):
            made = made * jnp.where(o < c, dec_s[o, 0:1, lanes], 1.0)
        return made

    def gated(rows, quad):
        lanes = slice(quad * 256, (quad + 1) * 256)
        carried = nn(c_ref[rows, :], entry_s[:, lanes])
        g = p_s[rows, lanes] + q_s[rows, lanes] * carried
        high, low = split2(g * g)
        mean = nn(high, block) + nn(low, block)
        normed_s[:, lanes] = (g * lax.rsqrt(mean + EPS) * gain_ref[:, lanes]).astype(BF16)

    def project(index):
        for n in range(width_out // 256):
            cols = slice(n * 256, (n + 1) * 256)
            made = nn(normed_s[...], w_s[:, cols]).astype(BF16)
            for u in range(per_chunk):
                mine_s[index * per_chunk + u, :, cols] = made[u * piece : (u + 1) * piece, :]
        for u in range(per_chunk):
            j = index * per_chunk + u

            @pl.when(j != band)
            def _(j=j):
                send(j).start()

    def rows_of(index):
        return pl.ds(pl.multiple_of(index * chunk, chunk), chunk)

    for side in range(2):
        base = (1 - mine_half if side == 0 else mine_half) * half
        c = base * chunk // GROUP
        if side == 0:
            for j in range(batches):
                for q in others():
                    enter_copy(j, q, q).wait_recv()
                entry_of(c, j)
            load_w.wait()
        else:
            for j in range(batches):
                entry_of(c, j)

        @pl.loop(0, half)
        def _(i, base=base, side=side):
            index = base + lax.rem(turn + i + side, half)
            for quad in range(quads):
                gated(rows_of(index), quad)
            project(index)

    keep = pltpu.make_async_copy(mine_s.at[band], out_hbm.at[band], sem_o)
    keep.start()
    for q in others():
        note_copy(q, me).wait_send()
        for j in range(batches):
            state_copy(j, q, me).wait_send()
            enter_copy(j, q, me).wait_send()
    later(lambda k, g: aggnote_copy(k, g).wait_send())
    for j in range(batches):
        later(lambda k, g: agg_copy(j, k, g).wait_send())
    for d in range(1, bands):
        arrival(lax.rem(band - d + bands, bands)).wait_recv()
    for d in range(1, bands):
        send(lax.rem(band + d, bands)).wait_send()
    keep.wait()


def CUTS(pairs):
    return [0, pairs // 2, pairs * 3 // 4, pairs]


def mixer_part(order, skip, b, c, ld, gain, x, gate, w, views, bands):
    heads, tokens = ld.shape
    width, width_out = w.shape
    pack = 2 if bands % 2 == 0 and heads % (4 * views) == 0 else 1
    count = views * pack
    batches = heads // (2 * count)
    groups = bands // pack
    piece = tokens // bands
    spans = tokens // GROUP
    vmem = pl.BlockSpec(memory_space=pltpu.VMEM)
    hbm = pl.BlockSpec(memory_space=pl.ANY)
    smem = pl.BlockSpec(memory_space=pltpu.SMEM)
    dma = pltpu.SemaphoreType.DMA
    sems = lambda *n: dma(n)
    return pl.pallas_call(
        functools.partial(mixer_kernel, views, pack, groups, batches, bands),
        in_specs=[smem] * 2 + [vmem] * 4 + [hbm] * 3,
        out_specs=hbm,
        out_shape=jax.ShapeDtypeStruct((bands, piece, width_out), BF16),
        scratch_shapes=[
            VMEM(x.shape, BF16),
            VMEM(x.shape, BF16),
            VMEM(w.shape, BF16),
            VMEM(x.shape, F32),
            VMEM(x.shape, F32),
            dma, dma, dma, dma,
            VMEM((tokens, 128), F32),
            VMEM((heads, tokens), F32),
            VMEM((spans, GROUP, GROUP), F32),
            VMEM((128, tokens), BF16),
            VMEM((tokens, 256), BF16),
            VMEM((tokens, 256), BF16),
            VMEM((spans, 8, width), F32),
            VMEM((heads, 128), F32),
            VMEM((spans, 128, width), F32),
            VMEM((count, 8, 128), F32),
            VMEM((count, 8, 128), F32),
            VMEM((8, 128), F32),
            VMEM((groups, 8, 128), F32),
            VMEM((count, count, 8, 128), F32),
            VMEM((count, 8, 128), F32),
            VMEM((count, 8, 128), F32),
            VMEM((batches, count, 128, 128), BF16),
            VMEM((batches, count, 128, 128), BF16),
            VMEM((batches, 128, 128), BF16),
            VMEM((batches, groups, 128, 128), BF16),
            VMEM((batches, count, 128, 128), F32),
            VMEM((128, 128), F32),
            VMEM((batches, count, 128, 128), BF16),
            VMEM((batches, count, 128, 128), BF16),
            sems(2, count), sems(batches, 2, count), sems(2, groups),
            sems(batches, 2, groups), sems(batches, 2, count),
            VMEM((128, width), BF16),
            VMEM((max(piece, TILE // 2), width), BF16),
            VMEM((bands, piece, width_out), BF16),
            sems(2, bands),
        ],
        compiler_params=pltpu.CompilerParams(
            collective_id=0, has_side_effects=True, vmem_limit_bytes=VMEM_LIMIT
        ),
        name="mixer_part",
    )(order, skip, b, c, ld, gain, x, gate, w)


def tile_kernel(order_ref, in_hbm, out_hbm, hold, sems):
    bands = in_hbm.shape[0]
    tiles, per = order_ref.shape[0], bands // order_ref.shape[0]

    def fetch(k):
        return pltpu.make_async_copy(
            in_hbm.at[pl.ds(order_ref[k] * per, per)], hold.at[k], sems.at[0, k]
        )

    def put(k):
        return pltpu.make_async_copy(
            hold.at[k], out_hbm.at[k * per : (k + 1) * per], sems.at[1, k]
        )

    for k in range(tiles):
        fetch(k).start()
    for k in range(tiles):
        fetch(k).wait()
        put(k).start()
    for k in range(tiles):
        put(k).wait()


def tile_part(order, pieces):
    bands, piece, width = pieces.shape
    tiles = order.shape[0]
    per = TILE // piece
    return pl.pallas_call(
        tile_kernel,
        in_specs=[
            pl.BlockSpec(memory_space=pltpu.SMEM),
            pl.BlockSpec(memory_space=pl.ANY),
        ],
        out_specs=pl.BlockSpec(memory_space=pl.ANY),
        out_shape=jax.ShapeDtypeStruct(pieces.shape, BF16),
        scratch_shapes=[
            VMEM((tiles, per, piece, width), BF16),
            pltpu.SemaphoreType.DMA((2, tiles)),
        ],
        compiler_params=pltpu.CompilerParams(vmem_limit_bytes=VMEM_LIMIT),
        name="tile_part",
    )(order, pieces)


def shards(
    ssd_input, gate_input, b_matrix, c_matrix, log_decay,
    d_skip, norm_gain, out_weight, view_order, tile_order,
):
    views, bands = lax.axis_size("view"), lax.axis_size("seq")
    x, gate = ssd_input[0, 0], gate_input[0, 0]
    b, c, ld = b_matrix[0, 0], c_matrix[0, 0], log_decay[0, 0]
    tokens, width = x.shape
    pieces = mixer_part(
        view_order, d_skip, b, c, ld, norm_gain[None, :], x, gate, out_weight, views, bands
    )
    out = tile_part(tile_order[0], pieces)
    return out.reshape(1, 1, tokens, out_weight.shape[1])


def solution(mesh):
    whole = P("seq", "view", None, None)
    in_specs = (whole,) * 5 + (P(), P(), P(), P("seq", None), P("seq", None))
    return jax.shard_map(
        shards, mesh=mesh, in_specs=in_specs, out_specs=whole, check_vma=False
    )
```

```python
import functools
import math

import jax
import jax.numpy as jnp
from jax import lax
from jax.experimental import pallas as pl
from jax.experimental.pallas import tpu as pltpu
from jax.sharding import PartitionSpec as P

GROUP = 256
TILE = 128
EPS = 1e-05
LOG2E = math.log2(math.e)
MESH = pl.DeviceIdType.MESH
F32 = jnp.float32
BF16 = jnp.bfloat16
VMEM = pltpu.VMEM
VMEM_LIMIT = 64 * 1000 * 1000


def nn(a, b):
    return lax.dot_general(a, b, (((1,), (0,)), ((), ())), preferred_element_type=F32)


def nt(a, b):
    return lax.dot_general(a, b, (((1,), (1,)), ((), ())), preferred_element_type=F32)


def split2(a):
    hi = a.astype(BF16)
    return hi, (a - hi.astype(F32)).astype(BF16)


def split3(a):
    hi = a.astype(BF16)
    rest = a - hi.astype(F32)
    mid = rest.astype(BF16)
    low = (rest - mid.astype(F32)).astype(BF16)
    return hi, mid, low


def iota(shape, dim):
    return lax.broadcasted_iota(jnp.int32, shape, dim)


def pair_columns(full, pair):
    lanes = full.shape[1]
    turned = pltpu.roll(full, lax.rem(lanes - 2 * pair, lanes), 1)
    return turned[:, 0:1], turned[:, 1:2]


def spread(first, width):
    row = iota((256, width), 0)
    head = jnp.where(row < 128, row, row - 128)
    return jnp.where(head == first + (iota((256, width), 1) >> 6), 1.0, 0.0).astype(BF16)


def mixer_kernel(
    views, pack, groups, batches, bands,
    order_ref, skip_ref, b_ref, c_ref, ld_ref, gain_ref, x_hbm, gate_hbm, w_hbm,
    out_hbm,
    x_s, gate_s, w_s, p_s, q_s, sem_x, sem_g, sem_w, sem_o,
    col_ref, row_ref, score_ref, bt_s, scale2_s, ecol2_s, dec_s, total_s, prefix_s,
    note_s, gotnote_s, aggnote_s, aggnotes_s, coef_s, before_s, last_s,
    state_s, got_s, agg_s, aggs_s, within_s, carry_s, send_s, ent_s,
    sem_n, sem_a, sem_bn, sem_b, sem_c,
    entry_s, normed_s, mine_s, sem,
):
    band, view = lax.axis_index("seq"), lax.axis_index("view")
    count = views * pack
    chips = count // 2
    group, member = band // pack, lax.rem(band, pack)
    me = member * views + view
    heads, tokens = ld_ref.shape
    spans = tokens // GROUP
    width = x_s.shape[1]
    pairs = width // 128
    HALF = GROUP // 2

    load = pltpu.make_async_copy(x_hbm, x_s, sem_x)
    load_gate = pltpu.make_async_copy(gate_hbm, gate_s, sem_g)
    load_w = pltpu.make_async_copy(w_hbm, w_s, sem_w)
    load.start()
    load_gate.start()
    load_w.start()

    barrier = pltpu.get_barrier_semaphore()
    for d in range(1, bands):
        pl.semaphore_signal(
            barrier, inc=1,
            device_id={"seq": lax.rem(band + d, bands), "view": view}, device_id_type=MESH,
        )
    for d in range(1, views):
        for m in range(pack):
            pl.semaphore_signal(
                barrier, inc=1,
                device_id={"seq": group * pack + m, "view": lax.rem(view + d, views)},
                device_id_type=MESH,
            )

    at_row, at_col = iota((GROUP, GROUP), 0), iota((GROUP, GROUP), 1)
    lower = jnp.where(at_col <= at_row, 1.0, 0.0).astype(BF16)
    upper = jnp.where(at_row <= at_col, 1.0, 0.0).astype(BF16)
    total = jnp.zeros((heads, 1), F32)
    for c in range(spans):
        span = slice(c * GROUP, (c + 1) * GROUP)
        own = ld_ref[:, span] * LOG2E
        padded = jnp.concatenate([own, jnp.zeros((128 - heads, GROUP), F32)], axis=0)
        lines = sum(nn(part, upper) for part in split3(own))
        row_ref[:, span] = lines
        cols = sum(nt(lower, part) for part in split3(padded))
        col_ref[span, :] = cols
        for ref, value in (
            (ecol2_s, jnp.exp2(cols)),
            (scale2_s, jnp.exp2(jnp.minimum(cols[GROUP - 1 : GROUP, :] - cols, 0.0))),
        ):
            hi, lo = split2(value)
            ref[span, 0:128] = hi
            ref[span, 128:256] = lo
        total = total + lines[:, GROUP - 1 : GROUP]
        bt_s[:, span] = b_ref[span, :].astype(F32).T.astype(BF16)
    total_s[...] = jnp.broadcast_to(total, total_s.shape)

    rank = jnp.int32(0)
    for r in range(views):
        rank = rank + jnp.where(order_ref[0, r] == view, r, 0)
    key = (rank + member * views).astype(F32)
    left = iota((1, 128), 1) < 64
    for q in range(count):
        for j in range(batches):
            head = 2 * (j * count + q)
            note_s[q, j : j + 1, :] = jnp.where(
                left, total_s[head : head + 1, :], total_s[head + 1 : head + 2, :]
            )
        note_s[q, batches : batches + 1, :] = jnp.full((1, 128), key, F32)

    def peer(q):
        return {"seq": group * pack + q // views, "view": lax.rem(q, views)}

    def exchange(source, target, sends, receives, q):
        return pltpu.make_async_remote_copy(
            src_ref=source, dst_ref=target, send_sem=sends, recv_sem=receives,
            device_id=peer(q), device_id_type=MESH,
        )

    def note_copy(q, slot):
        return exchange(note_s.at[q], gotnote_s.at[slot], sem_n.at[0, q], sem_n.at[1, slot], q)

    def state_copy(j, q, slot):
        return exchange(
            state_s.at[j, q], got_s.at[j, slot], sem_a.at[j, 0, q], sem_a.at[j, 1, slot], q
        )

    def enter_copy(j, q, slot):
        return exchange(
            send_s.at[j, q], ent_s.at[j, slot], sem_c.at[j, 0, q], sem_c.at[j, 1, slot], q
        )

    def others():
        return [lax.rem(me + d, count) for d in range(1, count)]

    def ahead(source, target, sems, k, g):
        return pltpu.make_async_remote_copy(
            src_ref=source, dst_ref=target, send_sem=sems.at[0, k], recv_sem=sems.at[1, k],
            device_id={"seq": g * pack + member, "view": view}, device_id_type=MESH,
        )

    def aggnote_copy(k, g):
        return ahead(aggnote_s, aggnotes_s.at[k], sem_bn, k, g)

    def agg_copy(j, k, g):
        return ahead(agg_s.at[j], aggs_s.at[j, k], sem_b.at[j], k, g)

    def later(run):
        for k in range(groups - 1, 0, -1):
            @pl.when(group + k < groups)
            def _(k=k):
                run(k, group + k)

    def earlier(run):
        for k in range(groups - 1, 0, -1):
            @pl.when(group - k >= 0)
            def _(k=k):
                run(k, group - k)

    pl.semaphore_wait(barrier, bands - 1 + (views - 1) * pack)
    for q in others():
        note_copy(q, me).start()

    def states(j, chip):
        base = j * count + 2 * chip
        lanes = pl.ds(pl.multiple_of(base * 128, 256), 256)
        pick = spread(2 * base, 256)
        running = jnp.zeros((128, 256), F32)
        for c in range(spans):
            span = slice(c * GROUP, (c + 1) * GROUP)
            scale = nn(scale2_s[span, :], pick)
            made = nn(bt_s[:, span], (x_s[span, lanes].astype(F32) * scale).astype(BF16))
            ends = nn(ecol2_s[(c + 1) * GROUP - 16 : (c + 1) * GROUP, :], pick)
            dec = ends[15:16, :]
            prefix_s[c, :, lanes] = running
            dec_s[c, :, lanes] = jnp.broadcast_to(dec, (8, 256))
            running = dec * running + made if c else made
        for i in range(2):
            state_s[j, 2 * chip + i] = running[:, i * 128 : (i + 1) * 128].astype(BF16)

    mychip = me // 2
    partner = me + 1 - 2 * lax.rem(me, 2)
    load.wait()
    for j in range(batches):
        for d in range(1, chips):
            chip = lax.rem(mychip + d, chips)
            states(j, chip)
            for i in range(2):
                state_copy(j, 2 * chip + i, me).start()
        states(j, mychip)
        state_copy(j, partner, me).start()
        got_s[j, me] = state_s[j, me]

    for c in range(spans):
        span = slice(c * GROUP, (c + 1) * GROUP)
        scores = nt(c_ref[span, :], b_ref[span, :])
        score_ref[c] = jnp.where(at_col <= at_row, scores, 0.0)

    first_half = iota((GROUP, 128), 1) < 64

    def inside_span(start, stop):
        @pl.loop(start, stop)
        def _(pair):
            cols = pair_columns(col_ref[...], pair)
            lanes = pl.ds(pl.multiple_of(pair * 128, 128), 128)
            pick = spread(2 * pair, 128)
            for c in range(spans):
                span = slice(c * GROUP, (c + 1) * GROUP)
                x = x_s[span, lanes]
                outs = []
                for j, col in enumerate(cols):
                    line = row_ref[pl.ds(2 * pair + j, 1), span]
                    col = col[span, :]
                    top = jnp.minimum(col[:HALF] - line[:, :HALF], 0.0)
                    top = (jnp.exp2(top) * score_ref[c, :HALF, :HALF]).astype(BF16)
                    low = jnp.minimum(col[HALF:] - line, 0.0)
                    low = (jnp.exp2(low) * score_ref[c, HALF:, :]).astype(BF16)
                    outs.append(jnp.concatenate([nn(top, x[:HALF]), nn(low, x)], axis=0))
                gate = gate_s[span, lanes].astype(F32)
                silu = gate / (1.0 + jnp.exp(-gate))
                q_s[span, lanes] = nn(ecol2_s[span, :], pick) * silu
                made = jnp.where(first_half, outs[0], outs[1]) + jnp.where(
                    first_half, skip_ref[2 * pair], skip_ref[2 * pair + 1]
                ) * x.astype(F32)
                p_s[span, lanes] = made * silu

    cuts = CUTS(pairs)
    load_gate.wait()
    inside_span(cuts[0], cuts[1])

    gotnote_s[me] = note_s[me]
    for q in others():
        note_copy(q, q).wait_recv()
    logs = [gotnote_s[b] for b in range(count)]
    keys = [jnp.broadcast_to(log[batches : batches + 1, :], log.shape) for log in logs]
    zero = jnp.zeros_like(logs[0])
    upto, whole = [], zero
    for b in range(count):
        acc = zero
        for o in range(count):
            if o != b:
                acc = acc + jnp.where(keys[o] < keys[b], logs[o], 0.0)
        upto.append(acc + logs[b])
        before_s[b] = jnp.exp2(acc)
        for o in range(count):
            coef_s[b, o] = acc
        whole = whole + logs[b]
    aggnote_s[...] = whole
    later(lambda k, g: aggnote_copy(k, g).start())
    for b in range(count):
        last_s[b] = jnp.exp2(jnp.minimum(whole - upto[b], 0.0))
        for o in range(count):
            if o != b:
                coef_s[b, o] = jnp.where(
                    keys[o] < keys[b], jnp.exp2(jnp.minimum(coef_s[b, o] - upto[o], 0.0)), 0.0
                )

    for j in range(batches):
        for q in others():
            state_copy(j, q, q).wait_recv()
        for i in range(4):
            part = slice(i * 32, (i + 1) * 32)
            acc = jnp.zeros((32, 128), F32)
            for b in range(count):
                acc = acc + last_s[b, j : j + 1, :] * got_s[j, b, part, :].astype(F32)
            agg_s[j, part, :] = acc.astype(BF16)
        later(lambda k, g: agg_copy(j, k, g).start())
        for i in range(4):
            part = slice(i * 32, (i + 1) * 32)
            blocks = [got_s[j, o, part, :].astype(F32) for o in range(count)]
            for b in range(count):
                acc = jnp.zeros((32, 128), F32)
                for o in range(count):
                    if o != b:
                        acc = acc + coef_s[b, o, j : j + 1, :] * blocks[o]
                within_s[j, b, part, :] = acc

    inside_span(cuts[1], cuts[2])

    earlier(lambda k, g: aggnote_copy(k, g).wait_recv())
    for j in range(batches):
        carry_s[...] = jnp.zeros_like(carry_s)

        def gather(k, g):
            agg_copy(j, k, g).wait_recv()
            decay = jnp.exp2(aggnotes_s[k, j : j + 1, :])
            carry_s[...] = decay * carry_s[...] + aggs_s[j, k].astype(F32)

        earlier(gather)

        def entering(q):
            return (before_s[q, j : j + 1, :] * carry_s[...] + within_s[j, q]).astype(BF16)

        for q in others():
            send_s[j, q] = entering(q)
            enter_copy(j, q, me).start()
        ent_s[j, me] = entering(me)

    inside_span(cuts[2], cuts[3])

    piece = mine_s.shape[1]
    width_out = w_s.shape[1]
    chunk = normed_s.shape[0]
    chunks = tokens // chunk
    half = chunks // 2
    per_chunk = chunk // piece
    turn = lax.rem(band // per_chunk, half)
    mine_half = band // (bands // 2)
    same = (iota((256, 256), 0) >> 6) == (iota((256, 256), 1) >> 6)
    block = jnp.where(same, 1.0 / 64.0, 0.0).astype(BF16)
    quads = width // 256

    def send(j):
        return pltpu.make_async_remote_copy(
            src_ref=mine_s.at[j], dst_ref=out_hbm.at[band],
            send_sem=sem.at[0, j], recv_sem=sem.at[1, band],
            device_id={"seq": j, "view": view}, device_id_type=MESH,
        )

    def arrival(i):
        return pltpu.make_async_remote_copy(
            src_ref=mine_s.at[i], dst_ref=out_hbm.at[i],
            send_sem=sem.at[0, i], recv_sem=sem.at[1, i],
            device_id={"seq": i, "view": view}, device_id_type=MESH,
        )

    def entry_of(c, j):
        for q in range(count):
            at = (j * count + q) * 128
            lanes = slice(at, at + 128)
            made = ent_s[j, q].astype(F32)
            entry_s[:, lanes] = (before_of(c, lanes) * made + prefix_s[c, :, lanes]).astype(BF16)

    def before_of(c, lanes):
        made = jnp.ones((1, lanes.stop - lanes.start), F32)
        for o in range(spans - 1):
            made = made * jnp.where(o < c, dec_s[o, 0:1, lanes], 1.0)
        return made

    def gated(rows, quad):
        lanes = slice(quad * 256, (quad + 1) * 256)
        carried = nn(c_ref[rows, :], entry_s[:, lanes])
        g = p_s[rows, lanes] + q_s[rows, lanes] * carried
        high, low = split2(g * g)
        mean = nn(high, block) + nn(low, block)
        normed_s[:, lanes] = (g * lax.rsqrt(mean + EPS) * gain_ref[:, lanes]).astype(BF16)

    def project(index):
        for n in range(width_out // 256):
            cols = slice(n * 256, (n + 1) * 256)
            made = nn(normed_s[...], w_s[:, cols]).astype(BF16)
            for u in range(per_chunk):
                mine_s[index * per_chunk + u, :, cols] = made[u * piece : (u + 1) * piece, :]
        for u in range(per_chunk):
            j = index * per_chunk + u

            @pl.when(j != band)
            def _(j=j):
                send(j).start()

    def rows_of(index):
        return pl.ds(pl.multiple_of(index * chunk, chunk), chunk)

    for side in range(2):
        base = (1 - mine_half if side == 0 else mine_half) * half
        c = base * chunk // GROUP
        if side == 0:
            for j in range(batches):
                for q in others():
                    enter_copy(j, q, q).wait_recv()
                entry_of(c, j)
            load_w.wait()
        else:
            for j in range(batches):
                entry_of(c, j)

        @pl.loop(0, half)
        def _(i, base=base, side=side):
            index = base + lax.rem(turn + i + side, half)
            for quad in range(quads):
                gated(rows_of(index), quad)
            project(index)

    keep = pltpu.make_async_copy(mine_s.at[band], out_hbm.at[band], sem_o)
    keep.start()
    for q in others():
        note_copy(q, me).wait_send()
        for j in range(batches):
            state_copy(j, q, me).wait_send()
            enter_copy(j, q, me).wait_send()
    later(lambda k, g: aggnote_copy(k, g).wait_send())
    for j in range(batches):
        later(lambda k, g: agg_copy(j, k, g).wait_send())
    for d in range(1, bands):
        arrival(lax.rem(band - d + bands, bands)).wait_recv()
    for d in range(1, bands):
        send(lax.rem(band + d, bands)).wait_send()
    keep.wait()


def CUTS(pairs):
    return [0, pairs // 2, pairs * 3 // 4, pairs]


def mixer_part(order, skip, b, c, ld, gain, x, gate, w, views, bands):
    heads, tokens = ld.shape
    width, width_out = w.shape
    pack = 2 if bands % 2 == 0 and heads % (4 * views) == 0 else 1
    count = views * pack
    batches = heads // (2 * count)
    groups = bands // pack
    piece = tokens // bands
    spans = tokens // GROUP
    vmem = pl.BlockSpec(memory_space=pltpu.VMEM)
    hbm = pl.BlockSpec(memory_space=pl.ANY)
    smem = pl.BlockSpec(memory_space=pltpu.SMEM)
    dma = pltpu.SemaphoreType.DMA
    sems = lambda *n: dma(n)
    return pl.pallas_call(
        functools.partial(mixer_kernel, views, pack, groups, batches, bands),
        in_specs=[smem] * 2 + [vmem] * 4 + [hbm] * 3,
        out_specs=vmem,
        out_shape=VMEM((bands, piece, width_out), BF16),
        scratch_shapes=[
            VMEM(x.shape, BF16),
            VMEM(x.shape, BF16),
            VMEM(w.shape, BF16),
            VMEM(x.shape, F32),
            VMEM(x.shape, F32),
            dma, dma, dma, dma,
            VMEM((tokens, 128), F32),
            VMEM((heads, tokens), F32),
            VMEM((spans, GROUP, GROUP), F32),
            VMEM((128, tokens), BF16),
            VMEM((tokens, 256), BF16),
            VMEM((tokens, 256), BF16),
            VMEM((spans, 8, width), F32),
            VMEM((heads, 128), F32),
            VMEM((spans, 128, width), F32),
            VMEM((count, 8, 128), F32),
            VMEM((count, 8, 128), F32),
            VMEM((8, 128), F32),
            VMEM((groups, 8, 128), F32),
            VMEM((count, count, 8, 128), F32),
            VMEM((count, 8, 128), F32),
            VMEM((count, 8, 128), F32),
            VMEM((batches, count, 128, 128), BF16),
            VMEM((batches, count, 128, 128), BF16),
            VMEM((batches, 128, 128), BF16),
            VMEM((batches, groups, 128, 128), BF16),
            VMEM((batches, count, 128, 128), F32),
            VMEM((128, 128), F32),
            VMEM((batches, count, 128, 128), BF16),
            VMEM((batches, count, 128, 128), BF16),
            sems(2, count), sems(batches, 2, count), sems(2, groups),
            sems(batches, 2, groups), sems(batches, 2, count),
            VMEM((128, width), BF16),
            VMEM((max(piece, TILE // 2), width), BF16),
            VMEM((bands, piece, width_out), BF16),
            sems(2, bands),
        ],
        compiler_params=pltpu.CompilerParams(
            collective_id=0, has_side_effects=True, vmem_limit_bytes=VMEM_LIMIT
        ),
        name="mixer_part",
    )(order, skip, b, c, ld, gain, x, gate, w)


def tile_kernel(order_ref, in_ref, out_hbm, sems):
    tiles = order_ref.shape[0]
    per = in_ref.shape[0] // tiles

    def put(k):
        return pltpu.make_async_copy(
            in_ref.at[pl.ds(order_ref[k] * per, per)],
            out_hbm.at[k * per : (k + 1) * per],
            sems.at[k],
        )

    for k in range(tiles):
        put(k).start()
    for k in range(tiles):
        put(k).wait()


def tile_part(order, pieces):
    bands, piece, width = pieces.shape
    tiles = order.shape[0]
    return pl.pallas_call(
        tile_kernel,
        in_specs=[
            pl.BlockSpec(memory_space=pltpu.SMEM),
            pl.BlockSpec(memory_space=pl.ANY),
        ],
        out_specs=pl.BlockSpec(memory_space=pl.ANY),
        out_shape=jax.ShapeDtypeStruct(pieces.shape, BF16),
        scratch_shapes=[pltpu.SemaphoreType.DMA((tiles,))],
        compiler_params=pltpu.CompilerParams(vmem_limit_bytes=VMEM_LIMIT // 16),
        name="tile_part",
    )(order, pieces)


def shards(
    ssd_input, gate_input, b_matrix, c_matrix, log_decay,
    d_skip, norm_gain, out_weight, view_order, tile_order,
):
    views, bands = lax.axis_size("view"), lax.axis_size("seq")
    x, gate = ssd_input[0, 0], gate_input[0, 0]
    b, c, ld = b_matrix[0, 0], c_matrix[0, 0], log_decay[0, 0]
    tokens, width = x.shape
    pieces = mixer_part(
        view_order, d_skip, b, c, ld, norm_gain[None, :], x, gate, out_weight, views, bands
    )
    out = tile_part(tile_order[0], pieces)
    return out.reshape(1, 1, tokens, out_weight.shape[1])


def solution(mesh):
    whole = P("seq", "view", None, None)
    in_specs = (whole,) * 5 + (P(), P(), P(), P("seq", None), P("seq", None))
    return jax.shard_map(
        shards, mesh=mesh, in_specs=in_specs, out_specs=whole, check_vma=False
    )
```

```python
import functools
import math

import jax
import jax.numpy as jnp
from jax import lax
from jax.experimental import pallas as pl
from jax.experimental.pallas import tpu as pltpu
from jax.sharding import PartitionSpec as P

GROUP = 256
TILE = 128
EPS = 1e-05
LOG2E = math.log2(math.e)
MESH = pl.DeviceIdType.MESH
F32 = jnp.float32
BF16 = jnp.bfloat16
VMEM = pltpu.VMEM
VMEM_LIMIT = 64 * 1000 * 1000


def nn(a, b):
    return lax.dot_general(a, b, (((1,), (0,)), ((), ())), preferred_element_type=F32)


def nt(a, b):
    return lax.dot_general(a, b, (((1,), (1,)), ((), ())), preferred_element_type=F32)


def split2(a):
    hi = a.astype(BF16)
    return hi, (a - hi.astype(F32)).astype(BF16)


def split3(a):
    hi = a.astype(BF16)
    rest = a - hi.astype(F32)
    mid = rest.astype(BF16)
    low = (rest - mid.astype(F32)).astype(BF16)
    return hi, mid, low


def iota(shape, dim):
    return lax.broadcasted_iota(jnp.int32, shape, dim)


def pair_columns(full, pair):
    lanes = full.shape[1]
    turned = pltpu.roll(full, lax.rem(lanes - 2 * pair, lanes), 1)
    return turned[:, 0:1], turned[:, 1:2]


def spread(first, width):
    row = iota((256, width), 0)
    head = jnp.where(row < 128, row, row - 128)
    return jnp.where(head == first + (iota((256, width), 1) >> 6), 1.0, 0.0).astype(BF16)


def mixer_kernel(
    views, pack, groups, batches, bands,
    order_ref, skip_ref, b_ref, c_ref, ld_ref, gain_ref, x_hbm, gate_hbm, w_hbm,
    out_hbm,
    x_s, gate_s, w_s, p_s, q_s, sem_x, sem_g, sem_w, sem_o,
    col_ref, row_ref, score_ref, bt_s, scale2_s, ecol2_s, dec_s, total_s, prefix_s,
    note_s, gotnote_s, aggnote_s, aggnotes_s, coef_s, before_s, last_s,
    state_s, got_s, agg_s, aggs_s, within_s, carry_s, send_s, ent_s,
    sem_n, sem_a, sem_bn, sem_b, sem_c, pre_s, pregot_s, sem_p,
    entry_s, normed_s, made_s, mine_s, sem,
):
    band, view = lax.axis_index("seq"), lax.axis_index("view")
    count = views * pack
    chips = count // 2
    group, member = band // pack, lax.rem(band, pack)
    me = member * views + view
    heads, tokens = ld_ref.shape
    spans = tokens // GROUP
    width = x_s.shape[1]
    pairs = width // 128
    HALF = GROUP // 2

    load = pltpu.make_async_copy(x_hbm, x_s, sem_x)
    load_gate = pltpu.make_async_copy(gate_hbm, gate_s, sem_g)
    load_w = pltpu.make_async_copy(w_hbm, w_s, sem_w)
    load.start()
    load_gate.start()
    load_w.start()

    barrier = pltpu.get_barrier_semaphore()
    for d in range(1, bands):
        pl.semaphore_signal(
            barrier, inc=1,
            device_id={"seq": lax.rem(band + d, bands), "view": view}, device_id_type=MESH,
        )
    for d in range(1, views):
        for m in range(pack):
            pl.semaphore_signal(
                barrier, inc=1,
                device_id={"seq": group * pack + m, "view": lax.rem(view + d, views)},
                device_id_type=MESH,
            )

    at_row, at_col = iota((GROUP, GROUP), 0), iota((GROUP, GROUP), 1)
    lower = jnp.where(at_col <= at_row, 1.0, 0.0).astype(BF16)
    upper = jnp.where(at_row <= at_col, 1.0, 0.0).astype(BF16)
    total = jnp.zeros((heads, 1), F32)
    for c in range(spans):
        span = slice(c * GROUP, (c + 1) * GROUP)
        own = ld_ref[:, span] * LOG2E
        padded = jnp.concatenate([own, jnp.zeros((128 - heads, GROUP), F32)], axis=0)
        lines = sum(nn(part, upper) for part in split3(own))
        row_ref[:, span] = lines
        cols = sum(nt(lower, part) for part in split3(padded))
        col_ref[span, :] = cols
        for ref, value in (
            (ecol2_s, jnp.exp2(cols)),
            (scale2_s, jnp.exp2(jnp.minimum(cols[GROUP - 1 : GROUP, :] - cols, 0.0))),
        ):
            hi, lo = split2(value)
            ref[span, 0:128] = hi
            ref[span, 128:256] = lo
        total = total + lines[:, GROUP - 1 : GROUP]
        bt_s[:, span] = b_ref[span, :].astype(F32).T.astype(BF16)
    total_s[...] = jnp.broadcast_to(total, total_s.shape)

    rank = jnp.int32(0)
    for r in range(views):
        rank = rank + jnp.where(order_ref[0, r] == view, r, 0)
    key = (rank + member * views).astype(F32)
    left = iota((1, 128), 1) < 64
    for q in range(count):
        for j in range(batches):
            head = 2 * (j * count + q)
            note_s[q, j : j + 1, :] = jnp.where(
                left, total_s[head : head + 1, :], total_s[head + 1 : head + 2, :]
            )
        note_s[q, batches : batches + 1, :] = jnp.full((1, 128), key, F32)

    def peer(q):
        return {"seq": group * pack + q // views, "view": lax.rem(q, views)}

    def exchange(source, target, sends, receives, q):
        return pltpu.make_async_remote_copy(
            src_ref=source, dst_ref=target, send_sem=sends, recv_sem=receives,
            device_id=peer(q), device_id_type=MESH,
        )

    def note_copy(q, slot):
        return exchange(note_s.at[q], gotnote_s.at[slot], sem_n.at[0, q], sem_n.at[1, slot], q)

    def state_copy(j, q, slot):
        return exchange(
            state_s.at[j, q], got_s.at[j, slot], sem_a.at[j, 0, q], sem_a.at[j, 1, slot], q
        )

    def enter_copy(j, q, slot):
        return exchange(
            send_s.at[j, q], ent_s.at[j, slot], sem_c.at[j, 0, q], sem_c.at[j, 1, slot], q
        )

    mychip = me // 2
    partner = me + 1 - 2 * lax.rem(me, 2)

    def far_chips():
        if chips == 4:
            return [3 - mychip, lax.rem(mychip + 2, 4), mychip + 1 - 2 * lax.rem(mychip, 2)]
        return [lax.rem(mychip + d, chips) for d in range(1, chips)]

    def others():
        return [2 * chip + i for chip in far_chips() for i in range(2)] + [partner]

    def ahead(source, target, sems, k, g):
        return pltpu.make_async_remote_copy(
            src_ref=source, dst_ref=target, send_sem=sems.at[0, k], recv_sem=sems.at[1, k],
            device_id={"seq": g * pack + member, "view": view}, device_id_type=MESH,
        )

    def aggnote_copy(k, g):
        return ahead(aggnote_s, aggnotes_s.at[k], sem_bn, k, g)

    def agg_copy(j, k, g):
        return ahead(agg_s.at[j], aggs_s.at[j, k], sem_b.at[j], k, g)

    even = lax.rem(group, 2) == 0

    def later(run):
        for k in range(groups - 1, 0, -1):
            @pl.when((group + k < groups) & (lax.rem(group + k, 2) == 0))
            def _(k=k):
                run(k, group + k)

    def earlier(run):
        for k in range(groups - 1, 0, -1):
            @pl.when((group - k >= 0) & even)
            def _(k=k):
                run(k, group - k)

    def prefix_copy(j, g):
        return pltpu.make_async_remote_copy(
            src_ref=pre_s.at[j], dst_ref=pregot_s.at[j],
            send_sem=sem_p.at[0, j], recv_sem=sem_p.at[1, j],
            device_id={"seq": g * pack + member, "view": view}, device_id_type=MESH,
        )

    pl.semaphore_wait(barrier, bands - 1 + (views - 1) * pack)
    for q in others():
        note_copy(q, me).start()

    def states(j, chip):
        base = j * count + 2 * chip
        lanes = pl.ds(pl.multiple_of(base * 128, 256), 256)
        pick = spread(2 * base, 256)
        running = jnp.zeros((128, 256), F32)
        for c in range(spans):
            span = slice(c * GROUP, (c + 1) * GROUP)
            scale = nn(scale2_s[span, :], pick)
            made = nn(bt_s[:, span], (x_s[span, lanes].astype(F32) * scale).astype(BF16))
            ends = nn(ecol2_s[(c + 1) * GROUP - 16 : (c + 1) * GROUP, :], pick)
            dec = ends[15:16, :]
            prefix_s[c, :, lanes] = running
            dec_s[c, :, lanes] = jnp.broadcast_to(dec, (8, 256))
            running = dec * running + made if c else made
        for i in range(2):
            state_s[j, 2 * chip + i] = running[:, i * 128 : (i + 1) * 128].astype(BF16)

    load.wait()
    for j in range(batches):
        for chip in far_chips():
            states(j, chip)
            for i in range(2):
                state_copy(j, 2 * chip + i, me).start()
        states(j, mychip)
        state_copy(j, partner, me).start()
        got_s[j, me] = state_s[j, me]

    for c in range(spans):
        span = slice(c * GROUP, (c + 1) * GROUP)
        scores = nt(c_ref[span, :], b_ref[span, :])
        score_ref[c] = jnp.where(at_col <= at_row, scores, 0.0)

    first_half = iota((GROUP, 128), 1) < 64

    def inside_span(start, stop):
        @pl.loop(start, stop)
        def _(pair):
            cols = pair_columns(col_ref[...], pair)
            lanes = pl.ds(pl.multiple_of(pair * 128, 128), 128)
            pick = spread(2 * pair, 128)
            for c in range(spans):
                span = slice(c * GROUP, (c + 1) * GROUP)
                x = x_s[span, lanes]
                outs = []
                for j, col in enumerate(cols):
                    line = row_ref[pl.ds(2 * pair + j, 1), span]
                    col = col[span, :]
                    top = jnp.minimum(col[:HALF] - line[:, :HALF], 0.0)
                    top = (jnp.exp2(top) * score_ref[c, :HALF, :HALF]).astype(BF16)
                    low = jnp.minimum(col[HALF:] - line, 0.0)
                    low = (jnp.exp2(low) * score_ref[c, HALF:, :]).astype(BF16)
                    outs.append(jnp.concatenate([nn(top, x[:HALF]), nn(low, x)], axis=0))
                gate = gate_s[span, lanes].astype(F32)
                silu = gate / (1.0 + jnp.exp(-gate))
                q_s[span, lanes] = nn(ecol2_s[span, :], pick) * silu
                made = jnp.where(first_half, outs[0], outs[1]) + jnp.where(
                    first_half, skip_ref[2 * pair], skip_ref[2 * pair + 1]
                ) * x.astype(F32)
                p_s[span, lanes] = made * silu

    cuts = CUTS(pairs)
    load_gate.wait()
    inside_span(cuts[0], cuts[1])

    gotnote_s[me] = note_s[me]
    for q in others():
        note_copy(q, q).wait_recv()
    logs = [gotnote_s[b] for b in range(count)]
    keys = [jnp.broadcast_to(log[batches : batches + 1, :], log.shape) for log in logs]
    zero = jnp.zeros_like(logs[0])
    upto, whole = [], zero
    for b in range(count):
        acc = zero
        for o in range(count):
            if o != b:
                acc = acc + jnp.where(keys[o] < keys[b], logs[o], 0.0)
        upto.append(acc + logs[b])
        before_s[b] = jnp.exp2(acc)
        for o in range(count):
            coef_s[b, o] = acc
        whole = whole + logs[b]
    aggnote_s[...] = whole
    later(lambda k, g: aggnote_copy(k, g).start())
    for b in range(count):
        last_s[b] = jnp.exp2(jnp.minimum(whole - upto[b], 0.0))
        for o in range(count):
            if o != b:
                coef_s[b, o] = jnp.where(
                    keys[o] < keys[b], jnp.exp2(jnp.minimum(coef_s[b, o] - upto[o], 0.0)), 0.0
                )

    for j in range(batches):
        for q in others():
            state_copy(j, q, q).wait_recv()
        for i in range(4):
            part = slice(i * 32, (i + 1) * 32)
            acc = jnp.zeros((32, 128), F32)
            for b in range(count):
                acc = acc + last_s[b, j : j + 1, :] * got_s[j, b, part, :].astype(F32)
            agg_s[j, part, :] = acc.astype(BF16)
        later(lambda k, g: agg_copy(j, k, g).start())
        for i in range(4):
            part = slice(i * 32, (i + 1) * 32)
            blocks = [got_s[j, o, part, :].astype(F32) for o in range(count)]
            for b in range(count):
                acc = jnp.zeros((32, 128), F32)
                for o in range(count):
                    if o != b:
                        acc = acc + coef_s[b, o, j : j + 1, :] * blocks[o]
                within_s[j, b, part, :] = acc

    inside_span(cuts[1], cuts[2])

    earlier(lambda k, g: aggnote_copy(k, g).wait_recv())
    for j in range(batches):
        carry_s[...] = jnp.zeros_like(carry_s)

        def gather(k, g):
            agg_copy(j, k, g).wait_recv()
            decay = jnp.exp2(aggnotes_s[k, j : j + 1, :])
            carry_s[...] = decay * carry_s[...] + aggs_s[j, k].astype(F32)

        earlier(gather)

        @pl.when(jnp.logical_not(even))
        def _(j=j):
            prefix_copy(j, group - 1).wait_recv()
            carry_s[...] = pregot_s[j].astype(F32)

        @pl.when(even & (group + 1 < groups))
        def _(j=j):
            decay = jnp.exp2(aggnote_s[j : j + 1, :])
            pre_s[j] = (decay * carry_s[...] + agg_s[j].astype(F32)).astype(BF16)
            prefix_copy(j, group + 1).start()

        def entering(q):
            return (before_s[q, j : j + 1, :] * carry_s[...] + within_s[j, q]).astype(BF16)

        for q in others():
            send_s[j, q] = entering(q)
            enter_copy(j, q, me).start()
        ent_s[j, me] = entering(me)

    inside_span(cuts[2], cuts[3])

    piece = mine_s.shape[1]
    width_out = w_s.shape[1]
    chunk = normed_s.shape[0]
    chunks = tokens // chunk
    half = chunks // 2
    per_chunk = chunk // piece
    turn = lax.rem(band // per_chunk, half)
    mine_half = band // (bands // 2)

    def far_index(i):
        pair = i // 2
        f = (1 - mine_half) * (half // 2 - 1 - pair) + mine_half * pair
        return (1 - mine_half) * half + 2 * f + lax.rem(turn + i, 2)

    def near_index(i):
        return mine_half * half + lax.rem(turn + 1 + i, half)
    same = (iota((256, 256), 0) >> 6) == (iota((256, 256), 1) >> 6)
    block = jnp.where(same, 1.0 / 64.0, 0.0).astype(BF16)
    quads = width // 256

    def send(j):
        return pltpu.make_async_remote_copy(
            src_ref=mine_s.at[j], dst_ref=out_hbm.at[band],
            send_sem=sem.at[0, j], recv_sem=sem.at[1, band],
            device_id={"seq": j, "view": view}, device_id_type=MESH,
        )

    def arrival(i):
        return pltpu.make_async_remote_copy(
            src_ref=mine_s.at[i], dst_ref=out_hbm.at[i],
            send_sem=sem.at[0, i], recv_sem=sem.at[1, i],
            device_id={"seq": i, "view": view}, device_id_type=MESH,
        )

    def entry_of(c, j):
        for q in range(count):
            at = (j * count + q) * 128
            lanes = slice(at, at + 128)
            made = ent_s[j, q].astype(F32)
            entry_s[:, lanes] = (before_of(c, lanes) * made + prefix_s[c, :, lanes]).astype(BF16)

    def before_of(c, lanes):
        made = jnp.ones((1, lanes.stop - lanes.start), F32)
        for o in range(spans - 1):
            made = made * jnp.where(o < c, dec_s[o, 0:1, lanes], 1.0)
        return made

    def gated(rows, quad):
        lanes = slice(quad * 256, (quad + 1) * 256)
        carried = nn(c_ref[rows, :], entry_s[:, lanes])
        g = p_s[rows, lanes] + q_s[rows, lanes] * carried
        high, low = split2(g * g)
        mean = nn(high, block) + nn(low, block)
        normed_s[:, lanes] = (g * lax.rsqrt(mean + EPS) * gain_ref[:, lanes]).astype(BF16)

    def project(index, split=0):
        for n in range(width_out // 256):
            cols = slice(n * 256, (n + 1) * 256)
            made = nn(normed_s[:, split:], w_s[split:, cols])
            if split:
                made = made + made_s[:, cols]
            made = made.astype(BF16)
            for u in range(per_chunk):
                mine_s[index * per_chunk + u, :, cols] = made[u * piece : (u + 1) * piece, :]
        for u in range(per_chunk):
            j = index * per_chunk + u

            @pl.when(j != band)
            def _(j=j):
                send(j).start()

    def rows_of(index):
        return pl.ds(pl.multiple_of(index * chunk, chunk), chunk)

    lead = quads // batches
    split = (batches - 1) * lead * 256
    first = far_index(0)
    c = first * chunk // GROUP
    for j in range(batches):
        for q in others():
            enter_copy(j, q, q).wait_recv()
        entry_of(c, j)
        for quad in range(j * lead, (j + 1) * lead):
            gated(rows_of(first), quad)
        if j == batches - 2:
            load_w.wait()
            for n in range(width_out // 256):
                cols = slice(n * 256, (n + 1) * 256)
                made_s[:, cols] = nn(normed_s[:, :split], w_s[:split, cols])
    if batches == 1:
        load_w.wait()
    project(first, split)

    @pl.loop(1, half)
    def _(i):
        index = far_index(i)
        for quad in range(quads):
            gated(rows_of(index), quad)
        project(index)

    for j in range(batches):
        entry_of(mine_half * half * chunk // GROUP, j)

    @pl.loop(0, half)
    def _(i):
        index = near_index(i)
        for quad in range(quads):
            gated(rows_of(index), quad)
        project(index)

    keep = pltpu.make_async_copy(mine_s.at[band], out_hbm.at[band], sem_o)
    keep.start()
    for q in others():
        note_copy(q, me).wait_send()
        for j in range(batches):
            state_copy(j, q, me).wait_send()
            enter_copy(j, q, me).wait_send()
    later(lambda k, g: aggnote_copy(k, g).wait_send())
    for j in range(batches):
        later(lambda k, g: agg_copy(j, k, g).wait_send())

        @pl.when(even & (group + 1 < groups))
        def _(j=j):
            prefix_copy(j, group + 1).wait_send()

    for d in range(1, bands):
        arrival(lax.rem(band - d + bands, bands)).wait_recv()
    for d in range(1, bands):
        send(lax.rem(band + d, bands)).wait_send()
    keep.wait()


def CUTS(pairs):
    return [0, pairs // 2, pairs * 3 // 4, pairs]


def mixer_part(order, skip, b, c, ld, gain, x, gate, w, views, bands):
    heads, tokens = ld.shape
    width, width_out = w.shape
    pack = 2 if bands % 2 == 0 and heads % (4 * views) == 0 else 1
    count = views * pack
    batches = heads // (2 * count)
    groups = bands // pack
    piece = tokens // bands
    spans = tokens // GROUP
    vmem = pl.BlockSpec(memory_space=pltpu.VMEM)
    hbm = pl.BlockSpec(memory_space=pl.ANY)
    smem = pl.BlockSpec(memory_space=pltpu.SMEM)
    dma = pltpu.SemaphoreType.DMA
    sems = lambda *n: dma(n)
    return pl.pallas_call(
        functools.partial(mixer_kernel, views, pack, groups, batches, bands),
        in_specs=[smem] * 2 + [vmem] * 4 + [hbm] * 3,
        out_specs=vmem,
        out_shape=VMEM((bands, piece, width_out), BF16),
        scratch_shapes=[
            VMEM(x.shape, BF16),
            VMEM(x.shape, BF16),
            VMEM(w.shape, BF16),
            VMEM(x.shape, F32),
            VMEM(x.shape, F32),
            dma, dma, dma, dma,
            VMEM((tokens, 128), F32),
            VMEM((heads, tokens), F32),
            VMEM((spans, GROUP, GROUP), F32),
            VMEM((128, tokens), BF16),
            VMEM((tokens, 256), BF16),
            VMEM((tokens, 256), BF16),
            VMEM((spans, 8, width), F32),
            VMEM((heads, 128), F32),
            VMEM((spans, 128, width), F32),
            VMEM((count, 8, 128), F32),
            VMEM((count, 8, 128), F32),
            VMEM((8, 128), F32),
            VMEM((groups, 8, 128), F32),
            VMEM((count, count, 8, 128), F32),
            VMEM((count, 8, 128), F32),
            VMEM((count, 8, 128), F32),
            VMEM((batches, count, 128, 128), BF16),
            VMEM((batches, count, 128, 128), BF16),
            VMEM((batches, 128, 128), BF16),
            VMEM((batches, groups, 128, 128), BF16),
            VMEM((batches, count, 128, 128), F32),
            VMEM((128, 128), F32),
            VMEM((batches, count, 128, 128), BF16),
            VMEM((batches, count, 128, 128), BF16),
            sems(2, count), sems(batches, 2, count), sems(2, groups),
            sems(batches, 2, groups), sems(batches, 2, count),
            VMEM((batches, 128, 128), BF16),
            VMEM((batches, 128, 128), BF16),
            sems(2, batches),
            VMEM((128, width), BF16),
            VMEM((max(piece, TILE // 2), width), BF16),
            VMEM((max(piece, TILE // 2), width_out), F32),
            VMEM((bands, piece, width_out), BF16),
            sems(2, bands),
        ],
        compiler_params=pltpu.CompilerParams(
            collective_id=0, has_side_effects=True, vmem_limit_bytes=VMEM_LIMIT
        ),
        name="mixer_part",
    )(order, skip, b, c, ld, gain, x, gate, w)


def tile_kernel(order_ref, in_ref, out_hbm, sems):
    tiles = order_ref.shape[0]
    per = in_ref.shape[0] // tiles

    def put(k):
        return pltpu.make_async_copy(
            in_ref.at[pl.ds(order_ref[k] * per, per)],
            out_hbm.at[k * per : (k + 1) * per],
            sems.at[k],
        )

    for k in range(tiles):
        put(k).start()
    for k in range(tiles):
        put(k).wait()


def tile_part(order, pieces):
    bands, piece, width = pieces.shape
    tiles = order.shape[0]
    return pl.pallas_call(
        tile_kernel,
        in_specs=[
            pl.BlockSpec(memory_space=pltpu.SMEM),
            pl.BlockSpec(memory_space=pl.ANY),
        ],
        out_specs=pl.BlockSpec(memory_space=pl.ANY),
        out_shape=jax.ShapeDtypeStruct(pieces.shape, BF16),
        scratch_shapes=[pltpu.SemaphoreType.DMA((tiles,))],
        compiler_params=pltpu.CompilerParams(vmem_limit_bytes=VMEM_LIMIT // 16),
        name="tile_part",
    )(order, pieces)


def shards(
    ssd_input, gate_input, b_matrix, c_matrix, log_decay,
    d_skip, norm_gain, out_weight, view_order, tile_order,
):
    views, bands = lax.axis_size("view"), lax.axis_size("seq")
    x, gate = ssd_input[0, 0], gate_input[0, 0]
    b, c, ld = b_matrix[0, 0], c_matrix[0, 0], log_decay[0, 0]
    tokens, width = x.shape
    pieces = mixer_part(
        view_order, d_skip, b, c, ld, norm_gain[None, :], x, gate, out_weight, views, bands
    )
    out = tile_part(tile_order[0], pieces)
    return out.reshape(1, 1, tokens, out_weight.shape[1])


def solution(mesh):
    whole = P("seq", "view", None, None)
    in_specs = (whole,) * 5 + (P(), P(), P(), P("seq", None), P("seq", None))
    return jax.shard_map(
        shards, mesh=mesh, in_specs=in_specs, out_specs=whole, check_vma=False
    )
```

```python
import functools
import math

import jax
import jax.numpy as jnp
from jax import lax
from jax.experimental import pallas as pl
from jax.experimental.pallas import tpu as pltpu
from jax.sharding import PartitionSpec as P

GROUP = 256
TILE = 128
EPS = 1e-05
LOG2E = math.log2(math.e)
MESH = pl.DeviceIdType.MESH
F32 = jnp.float32
BF16 = jnp.bfloat16
VMEM = pltpu.VMEM
VMEM_LIMIT = 64 * 1000 * 1000


def nn(a, b):
    return lax.dot_general(a, b, (((1,), (0,)), ((), ())), preferred_element_type=F32)


def nt(a, b):
    return lax.dot_general(a, b, (((1,), (1,)), ((), ())), preferred_element_type=F32)


def split2(a):
    hi = a.astype(BF16)
    return hi, (a - hi.astype(F32)).astype(BF16)


def split3(a):
    hi = a.astype(BF16)
    rest = a - hi.astype(F32)
    mid = rest.astype(BF16)
    low = (rest - mid.astype(F32)).astype(BF16)
    return hi, mid, low


def iota(shape, dim):
    return lax.broadcasted_iota(jnp.int32, shape, dim)


def pair_columns(full, pair):
    lanes = full.shape[1]
    turned = pltpu.roll(full, lax.rem(lanes - 2 * pair, lanes), 1)
    return turned[:, 0:1], turned[:, 1:2]


def spread(first, width):
    row = iota((256, width), 0)
    head = jnp.where(row < 128, row, row - 128)
    return jnp.where(head == first + (iota((256, width), 1) >> 6), 1.0, 0.0).astype(BF16)


def mixer_kernel(
    views, pack, groups, batches, bands,
    order_ref, skip_ref, b_ref, c_ref, ld_ref, gain_ref, x_hbm, gate_hbm, w_hbm,
    out_hbm,
    x_s, gate_s, w_s, p_s, q_s, sem_x, sem_g, sem_w, sem_o,
    col_ref, row_ref, score_ref, bt_s, scale2_s, ecol2_s, dec_s, total_s, prefix_s,
    note_s, gotnote_s, aggnote_s, aggnotes_s, coef_s, before_s, last_s,
    state_s, got_s, agg_s, aggs_s, within_s, carry_s, send_s, ent_s,
    sem_n, sem_a, sem_bn, sem_b, sem_c, pre_s, pregot_s, sem_p,
    entry_s, normed_s, made_s, mine_s, sem,
):
    band, view = lax.axis_index("seq"), lax.axis_index("view")
    count = views * pack
    chips = count // 2
    group, member = band // pack, lax.rem(band, pack)
    me = member * views + view
    heads, tokens = ld_ref.shape
    spans = tokens // GROUP
    width = x_s.shape[1]
    pairs = width // 128
    HALF = GROUP // 2

    load = pltpu.make_async_copy(x_hbm, x_s, sem_x)
    load_gate = pltpu.make_async_copy(gate_hbm, gate_s, sem_g)
    load_w = pltpu.make_async_copy(w_hbm, w_s, sem_w)
    load.start()
    load_gate.start()
    load_w.start()

    barrier = pltpu.get_barrier_semaphore()
    for d in range(1, bands):
        pl.semaphore_signal(
            barrier, inc=1,
            device_id={"seq": lax.rem(band + d, bands), "view": view}, device_id_type=MESH,
        )
    for d in range(1, views):
        for m in range(pack):
            pl.semaphore_signal(
                barrier, inc=1,
                device_id={"seq": group * pack + m, "view": lax.rem(view + d, views)},
                device_id_type=MESH,
            )

    at_row, at_col = iota((GROUP, GROUP), 0), iota((GROUP, GROUP), 1)
    lower = jnp.where(at_col <= at_row, 1.0, 0.0).astype(BF16)
    upper = jnp.where(at_row <= at_col, 1.0, 0.0).astype(BF16)
    total = jnp.zeros((heads, 1), F32)
    for c in range(spans):
        span = slice(c * GROUP, (c + 1) * GROUP)
        own = ld_ref[:, span] * LOG2E
        padded = jnp.concatenate([own, jnp.zeros((128 - heads, GROUP), F32)], axis=0)
        lines = sum(nn(part, upper) for part in split3(own))
        row_ref[:, span] = lines
        cols = sum(nt(lower, part) for part in split3(padded))
        col_ref[span, :] = cols
        for ref, value in (
            (ecol2_s, jnp.exp2(cols)),
            (scale2_s, jnp.exp2(jnp.minimum(cols[GROUP - 1 : GROUP, :] - cols, 0.0))),
        ):
            hi, lo = split2(value)
            ref[span, 0:128] = hi
            ref[span, 128:256] = lo
        total = total + lines[:, GROUP - 1 : GROUP]
        bt_s[:, span] = b_ref[span, :].astype(F32).T.astype(BF16)
    total_s[...] = jnp.broadcast_to(total, total_s.shape)

    rank = jnp.int32(0)
    for r in range(views):
        rank = rank + jnp.where(order_ref[0, r] == view, r, 0)
    key = (rank + member * views).astype(F32)
    left = iota((1, 128), 1) < 64
    for q in range(count):
        for j in range(batches):
            head = 2 * (j * count + q)
            note_s[q, j : j + 1, :] = jnp.where(
                left, total_s[head : head + 1, :], total_s[head + 1 : head + 2, :]
            )
        note_s[q, batches : batches + 1, :] = jnp.full((1, 128), key, F32)

    def peer(q):
        return {"seq": group * pack + q // views, "view": lax.rem(q, views)}

    def exchange(source, target, sends, receives, q):
        return pltpu.make_async_remote_copy(
            src_ref=source, dst_ref=target, send_sem=sends, recv_sem=receives,
            device_id=peer(q), device_id_type=MESH,
        )

    def note_copy(q, slot):
        return exchange(note_s.at[q], gotnote_s.at[slot], sem_n.at[0, q], sem_n.at[1, slot], q)

    def state_copy(j, q, slot):
        return exchange(
            state_s.at[j, q], got_s.at[j, slot], sem_a.at[j, 0, q], sem_a.at[j, 1, slot], q
        )

    def enter_copy(j, q, slot):
        return exchange(
            send_s.at[j, q], ent_s.at[j, slot], sem_c.at[j, 0, q], sem_c.at[j, 1, slot], q
        )

    mychip = me // 2
    partner = me + 1 - 2 * lax.rem(me, 2)

    def far_chips():
        if chips == 4:
            return [3 - mychip, lax.rem(mychip + 2, 4), mychip + 1 - 2 * lax.rem(mychip, 2)]
        return [lax.rem(mychip + d, chips) for d in range(1, chips)]

    def others():
        return [2 * chip + i for chip in far_chips() for i in range(2)] + [partner]

    def ahead(source, target, sems, k, g):
        return pltpu.make_async_remote_copy(
            src_ref=source, dst_ref=target, send_sem=sems.at[0, k], recv_sem=sems.at[1, k],
            device_id={"seq": g * pack + member, "view": view}, device_id_type=MESH,
        )

    def aggnote_copy(k, g):
        return ahead(aggnote_s, aggnotes_s.at[k], sem_bn, k, g)

    def agg_copy(j, k, g):
        return ahead(agg_s.at[j], aggs_s.at[j, k], sem_b.at[j], k, g)

    even = lax.rem(group, 2) == 0

    def later(run):
        for k in range(groups - 1, 0, -1):
            @pl.when((group + k < groups) & (lax.rem(group + k, 2) == 0))
            def _(k=k):
                run(k, group + k)

    def earlier(run):
        for k in range(groups - 1, 0, -1):
            @pl.when((group - k >= 0) & even)
            def _(k=k):
                run(k, group - k)

    def prefix_copy(j, g):
        return pltpu.make_async_remote_copy(
            src_ref=pre_s.at[j], dst_ref=pregot_s.at[j],
            send_sem=sem_p.at[0, j], recv_sem=sem_p.at[1, j],
            device_id={"seq": g * pack + member, "view": view}, device_id_type=MESH,
        )

    pl.semaphore_wait(barrier, bands - 1 + (views - 1) * pack)
    for q in others():
        note_copy(q, me).start()

    def states(j, chip):
        base = j * count + 2 * chip
        lanes = pl.ds(pl.multiple_of(base * 128, 256), 256)
        pick = spread(2 * base, 256)
        running = jnp.zeros((128, 256), F32)
        for c in range(spans):
            span = slice(c * GROUP, (c + 1) * GROUP)
            scale = nn(scale2_s[span, :], pick)
            made = nn(bt_s[:, span], (x_s[span, lanes].astype(F32) * scale).astype(BF16))
            ends = nn(ecol2_s[(c + 1) * GROUP - 16 : (c + 1) * GROUP, :], pick)
            dec = ends[15:16, :]
            prefix_s[c, :, lanes] = running
            dec_s[c, :, lanes] = jnp.broadcast_to(dec, (8, 256))
            running = dec * running + made if c else made
        for i in range(2):
            state_s[j, 2 * chip + i] = running[:, i * 128 : (i + 1) * 128].astype(BF16)

    load.wait()
    for j in range(batches):
        for chip in far_chips():
            states(j, chip)
            for i in range(2):
                state_copy(j, 2 * chip + i, me).start()
        states(j, mychip)
        state_copy(j, partner, me).start()
        got_s[j, me] = state_s[j, me]

    for c in range(spans):
        span = slice(c * GROUP, (c + 1) * GROUP)
        scores = nt(c_ref[span, :], b_ref[span, :])
        score_ref[c] = jnp.where(at_col <= at_row, scores, 0.0)

    first_half = iota((GROUP, 128), 1) < 64

    def inside_span(start, stop):
        @pl.loop(start, stop)
        def _(pair):
            cols = pair_columns(col_ref[...], pair)
            lanes = pl.ds(pl.multiple_of(pair * 128, 128), 128)
            pick = spread(2 * pair, 128)
            for c in range(spans):
                span = slice(c * GROUP, (c + 1) * GROUP)
                x = x_s[span, lanes]
                outs = []
                for j, col in enumerate(cols):
                    line = row_ref[pl.ds(2 * pair + j, 1), span]
                    col = col[span, :]
                    top = jnp.minimum(col[:HALF] - line[:, :HALF], 0.0)
                    top = (jnp.exp2(top) * score_ref[c, :HALF, :HALF]).astype(BF16)
                    low = jnp.minimum(col[HALF:] - line, 0.0)
                    low = (jnp.exp2(low) * score_ref[c, HALF:, :]).astype(BF16)
                    outs.append(jnp.concatenate([nn(top, x[:HALF]), nn(low, x)], axis=0))
                gate = gate_s[span, lanes].astype(F32)
                silu = gate / (1.0 + jnp.exp(-gate))
                q_s[span, lanes] = nn(ecol2_s[span, :], pick) * silu
                made = jnp.where(first_half, outs[0], outs[1]) + jnp.where(
                    first_half, skip_ref[2 * pair], skip_ref[2 * pair + 1]
                ) * x.astype(F32)
                p_s[span, lanes] = made * silu

    cuts = fill_cuts(pairs, batches)
    load_gate.wait()
    inside_span(cuts[0], cuts[1])

    gotnote_s[me] = note_s[me]
    for q in others():
        note_copy(q, q).wait_recv()
    logs = [gotnote_s[b] for b in range(count)]
    keys = [jnp.broadcast_to(log[batches : batches + 1, :], log.shape) for log in logs]
    zero = jnp.zeros_like(logs[0])
    upto, whole = [], zero
    for b in range(count):
        acc = zero
        for o in range(count):
            if o != b:
                acc = acc + jnp.where(keys[o] < keys[b], logs[o], 0.0)
        upto.append(acc + logs[b])
        before_s[b] = jnp.exp2(acc)
        for o in range(count):
            coef_s[b, o] = acc
        whole = whole + logs[b]
    aggnote_s[...] = whole
    later(lambda k, g: aggnote_copy(k, g).start())
    for b in range(count):
        last_s[b] = jnp.exp2(jnp.minimum(whole - upto[b], 0.0))
        for o in range(count):
            if o != b:
                coef_s[b, o] = jnp.where(
                    keys[o] < keys[b], jnp.exp2(jnp.minimum(coef_s[b, o] - upto[o], 0.0)), 0.0
                )

    for j in range(batches):
        for q in others():
            state_copy(j, q, q).wait_recv()
        for i in range(4):
            part = slice(i * 32, (i + 1) * 32)
            acc = jnp.zeros((32, 128), F32)
            for b in range(count):
                acc = acc + last_s[b, j : j + 1, :] * got_s[j, b, part, :].astype(F32)
            agg_s[j, part, :] = acc.astype(BF16)
        later(lambda k, g: agg_copy(j, k, g).start())
        for i in range(4):
            part = slice(i * 32, (i + 1) * 32)
            blocks = [got_s[j, o, part, :].astype(F32) for o in range(count)]
            for b in range(count):
                acc = jnp.zeros((32, 128), F32)
                for o in range(count):
                    if o != b:
                        acc = acc + coef_s[b, o, j : j + 1, :] * blocks[o]
                within_s[j, b, part, :] = acc
        inside_span(cuts[j + 1], cuts[j + 2])

    earlier(lambda k, g: aggnote_copy(k, g).wait_recv())
    for j in range(batches):
        carry_s[...] = jnp.zeros_like(carry_s)

        def gather(k, g):
            agg_copy(j, k, g).wait_recv()
            decay = jnp.exp2(aggnotes_s[k, j : j + 1, :])
            carry_s[...] = decay * carry_s[...] + aggs_s[j, k].astype(F32)

        earlier(gather)

        @pl.when(jnp.logical_not(even))
        def _(j=j):
            prefix_copy(j, group - 1).wait_recv()
            carry_s[...] = pregot_s[j].astype(F32)

        @pl.when(even & (group + 1 < groups))
        def _(j=j):
            decay = jnp.exp2(aggnote_s[j : j + 1, :])
            pre_s[j] = (decay * carry_s[...] + agg_s[j].astype(F32)).astype(BF16)
            prefix_copy(j, group + 1).start()

        def entering(q):
            return (before_s[q, j : j + 1, :] * carry_s[...] + within_s[j, q]).astype(BF16)

        for q in others():
            send_s[j, q] = entering(q)
            enter_copy(j, q, me).start()
        ent_s[j, me] = entering(me)
        inside_span(cuts[batches + j + 1], cuts[batches + j + 2])

    piece = mine_s.shape[1]
    width_out = w_s.shape[1]
    chunk = normed_s.shape[0]
    chunks = tokens // chunk
    half = chunks // 2
    per_chunk = chunk // piece
    turn = lax.rem(band // per_chunk, half)
    mine_half = band // (bands // 2)

    def far_index(i):
        pair = i // 2
        f = (1 - mine_half) * (half // 2 - 1 - pair) + mine_half * pair
        return (1 - mine_half) * half + 2 * f + lax.rem(turn + i, 2)

    def near_index(i):
        return mine_half * half + lax.rem(turn + 1 + i, half)
    same = (iota((256, 256), 0) >> 6) == (iota((256, 256), 1) >> 6)
    block = jnp.where(same, 1.0 / 64.0, 0.0).astype(BF16)
    quads = width // 256

    def send(j):
        return pltpu.make_async_remote_copy(
            src_ref=mine_s.at[j], dst_ref=out_hbm.at[band],
            send_sem=sem.at[0, j], recv_sem=sem.at[1, band],
            device_id={"seq": j, "view": view}, device_id_type=MESH,
        )

    def arrival(i):
        return pltpu.make_async_remote_copy(
            src_ref=mine_s.at[i], dst_ref=out_hbm.at[i],
            send_sem=sem.at[0, i], recv_sem=sem.at[1, i],
            device_id={"seq": i, "view": view}, device_id_type=MESH,
        )

    def entry_of(c, j):
        for q in range(count):
            at = (j * count + q) * 128
            lanes = slice(at, at + 128)
            made = ent_s[j, q].astype(F32)
            entry_s[:, lanes] = (before_of(c, lanes) * made + prefix_s[c, :, lanes]).astype(BF16)

    def before_of(c, lanes):
        made = jnp.ones((1, lanes.stop - lanes.start), F32)
        for o in range(spans - 1):
            made = made * jnp.where(o < c, dec_s[o, 0:1, lanes], 1.0)
        return made

    def gated(rows, quad):
        lanes = slice(quad * 256, (quad + 1) * 256)
        carried = nn(c_ref[rows, :], entry_s[:, lanes])
        g = p_s[rows, lanes] + q_s[rows, lanes] * carried
        high, low = split2(g * g)
        mean = nn(high, block) + nn(low, block)
        normed_s[:, lanes] = (g * lax.rsqrt(mean + EPS) * gain_ref[:, lanes]).astype(BF16)

    def project(index, split=0):
        for n in range(width_out // 256):
            cols = slice(n * 256, (n + 1) * 256)
            made = nn(normed_s[:, split:], w_s[split:, cols])
            if split:
                made = made + made_s[:, cols]
            made = made.astype(BF16)
            for u in range(per_chunk):
                mine_s[index * per_chunk + u, :, cols] = made[u * piece : (u + 1) * piece, :]
        for u in range(per_chunk):
            j = index * per_chunk + u

            @pl.when(j != band)
            def _(j=j):
                send(j).start()

    def rows_of(index):
        return pl.ds(pl.multiple_of(index * chunk, chunk), chunk)

    lead = quads // batches
    split = (batches - 1) * lead * 256
    first = far_index(0)
    c = first * chunk // GROUP
    for j in range(batches):
        for q in others():
            enter_copy(j, q, q).wait_recv()
        entry_of(c, j)
        for quad in range(j * lead, (j + 1) * lead):
            gated(rows_of(first), quad)
        if j == batches - 2:
            load_w.wait()
            for n in range(width_out // 256):
                cols = slice(n * 256, (n + 1) * 256)
                made_s[:, cols] = nn(normed_s[:, :split], w_s[:split, cols])
    if batches == 1:
        load_w.wait()
    project(first, split)

    @pl.loop(1, half)
    def _(i):
        index = far_index(i)
        for quad in range(quads):
            gated(rows_of(index), quad)
        project(index)

    for j in range(batches):
        entry_of(mine_half * half * chunk // GROUP, j)

    @pl.loop(0, half)
    def _(i):
        index = near_index(i)
        for quad in range(quads):
            gated(rows_of(index), quad)
        project(index)

    keep = pltpu.make_async_copy(mine_s.at[band], out_hbm.at[band], sem_o)
    keep.start()
    for q in others():
        note_copy(q, me).wait_send()
        for j in range(batches):
            state_copy(j, q, me).wait_send()
            enter_copy(j, q, me).wait_send()
    later(lambda k, g: aggnote_copy(k, g).wait_send())
    for j in range(batches):
        later(lambda k, g: agg_copy(j, k, g).wait_send())

        @pl.when(even & (group + 1 < groups))
        def _(j=j):
            prefix_copy(j, group + 1).wait_send()

    for d in range(1, bands):
        arrival(lax.rem(band - d + bands, bands)).wait_recv()
    for d in range(1, bands):
        send(lax.rem(band + d, bands)).wait_send()
    keep.wait()


def fill_cuts(pairs, batches):
    shares = [4, 2, 1, 2, 7]
    if batches != 2:
        shares = [1] * (2 * batches + 1)
    return [pairs * sum(shares[:i]) // sum(shares) for i in range(len(shares) + 1)]


def mixer_part(order, skip, b, c, ld, gain, x, gate, w, views, bands):
    heads, tokens = ld.shape
    width, width_out = w.shape
    pack = 2 if bands % 2 == 0 and heads % (4 * views) == 0 else 1
    count = views * pack
    batches = heads // (2 * count)
    groups = bands // pack
    piece = tokens // bands
    spans = tokens // GROUP
    vmem = pl.BlockSpec(memory_space=pltpu.VMEM)
    hbm = pl.BlockSpec(memory_space=pl.ANY)
    smem = pl.BlockSpec(memory_space=pltpu.SMEM)
    dma = pltpu.SemaphoreType.DMA
    sems = lambda *n: dma(n)
    return pl.pallas_call(
        functools.partial(mixer_kernel, views, pack, groups, batches, bands),
        in_specs=[smem] * 2 + [vmem] * 4 + [hbm] * 3,
        out_specs=vmem,
        out_shape=VMEM((bands, piece, width_out), BF16),
        scratch_shapes=[
            VMEM(x.shape, BF16),
            VMEM(x.shape, BF16),
            VMEM(w.shape, BF16),
            VMEM(x.shape, F32),
            VMEM(x.shape, F32),
            dma, dma, dma, dma,
            VMEM((tokens, 128), F32),
            VMEM((heads, tokens), F32),
            VMEM((spans, GROUP, GROUP), F32),
            VMEM((128, tokens), BF16),
            VMEM((tokens, 256), BF16),
            VMEM((tokens, 256), BF16),
            VMEM((spans, 8, width), F32),
            VMEM((heads, 128), F32),
            VMEM((spans, 128, width), F32),
            VMEM((count, 8, 128), F32),
            VMEM((count, 8, 128), F32),
            VMEM((8, 128), F32),
            VMEM((groups, 8, 128), F32),
            VMEM((count, count, 8, 128), F32),
            VMEM((count, 8, 128), F32),
            VMEM((count, 8, 128), F32),
            VMEM((batches, count, 128, 128), BF16),
            VMEM((batches, count, 128, 128), BF16),
            VMEM((batches, 128, 128), BF16),
            VMEM((batches, groups, 128, 128), BF16),
            VMEM((batches, count, 128, 128), F32),
            VMEM((128, 128), F32),
            VMEM((batches, count, 128, 128), BF16),
            VMEM((batches, count, 128, 128), BF16),
            sems(2, count), sems(batches, 2, count), sems(2, groups),
            sems(batches, 2, groups), sems(batches, 2, count),
            VMEM((batches, 128, 128), BF16),
            VMEM((batches, 128, 128), BF16),
            sems(2, batches),
            VMEM((128, width), BF16),
            VMEM((max(piece, TILE // 2), width), BF16),
            VMEM((max(piece, TILE // 2), width_out), F32),
            VMEM((bands, piece, width_out), BF16),
            sems(2, bands),
        ],
        compiler_params=pltpu.CompilerParams(
            collective_id=0, has_side_effects=True, vmem_limit_bytes=VMEM_LIMIT
        ),
        name="mixer_part",
    )(order, skip, b, c, ld, gain, x, gate, w)


def tile_kernel(order_ref, in_ref, out_hbm, sems):
    tiles = order_ref.shape[0]
    per = in_ref.shape[0] // tiles

    def put(k):
        return pltpu.make_async_copy(
            in_ref.at[pl.ds(order_ref[k] * per, per)],
            out_hbm.at[k * per : (k + 1) * per],
            sems.at[k],
        )

    for k in range(tiles):
        put(k).start()
    for k in range(tiles):
        put(k).wait()


def tile_part(order, pieces):
    bands, piece, width = pieces.shape
    tiles = order.shape[0]
    return pl.pallas_call(
        tile_kernel,
        in_specs=[
            pl.BlockSpec(memory_space=pltpu.SMEM),
            pl.BlockSpec(memory_space=pl.ANY),
        ],
        out_specs=pl.BlockSpec(memory_space=pl.ANY),
        out_shape=jax.ShapeDtypeStruct(pieces.shape, BF16),
        scratch_shapes=[pltpu.SemaphoreType.DMA((tiles,))],
        compiler_params=pltpu.CompilerParams(vmem_limit_bytes=VMEM_LIMIT // 16),
        name="tile_part",
    )(order, pieces)


def shards(
    ssd_input, gate_input, b_matrix, c_matrix, log_decay,
    d_skip, norm_gain, out_weight, view_order, tile_order,
):
    views, bands = lax.axis_size("view"), lax.axis_size("seq")
    x, gate = ssd_input[0, 0], gate_input[0, 0]
    b, c, ld = b_matrix[0, 0], c_matrix[0, 0], log_decay[0, 0]
    tokens, width = x.shape
    pieces = mixer_part(
        view_order, d_skip, b, c, ld, norm_gain[None, :], x, gate, out_weight, views, bands
    )
    out = tile_part(tile_order[0], pieces)
    return out.reshape(1, 1, tokens, out_weight.shape[1])


def solution(mesh):
    whole = P("seq", "view", None, None)
    in_specs = (whole,) * 5 + (P(), P(), P(), P("seq", None), P("seq", None))
    return jax.shard_map(
        shards, mesh=mesh, in_specs=in_specs, out_specs=whole, check_vma=False
    )
```

```python
import functools
import math

import jax
import jax.numpy as jnp
from jax import lax
from jax.experimental import pallas as pl
from jax.experimental.pallas import tpu as pltpu
from jax.sharding import PartitionSpec as P

GROUP = 256
TILE = 128
EPS = 1e-05
LOG2E = math.log2(math.e)
MESH = pl.DeviceIdType.MESH
F32 = jnp.float32
BF16 = jnp.bfloat16
VMEM = pltpu.VMEM
VMEM_LIMIT = 64 * 1000 * 1000


def nn(a, b):
    return lax.dot_general(a, b, (((1,), (0,)), ((), ())), preferred_element_type=F32)


def nt(a, b):
    return lax.dot_general(a, b, (((1,), (1,)), ((), ())), preferred_element_type=F32)


def split2(a):
    hi = a.astype(BF16)
    return hi, (a - hi.astype(F32)).astype(BF16)


def split3(a):
    hi = a.astype(BF16)
    rest = a - hi.astype(F32)
    mid = rest.astype(BF16)
    low = (rest - mid.astype(F32)).astype(BF16)
    return hi, mid, low


def iota(shape, dim):
    return lax.broadcasted_iota(jnp.int32, shape, dim)


def pair_columns(full, pair):
    lanes = full.shape[1]
    turned = pltpu.roll(full, lax.rem(lanes - 2 * pair, lanes), 1)
    return turned[:, 0:1], turned[:, 1:2]


def spread(first, width):
    row = iota((256, width), 0)
    head = jnp.where(row < 128, row, row - 128)
    return jnp.where(head == first + (iota((256, width), 1) >> 6), 1.0, 0.0).astype(BF16)


def mixer_kernel(
    views, pack, groups, batches, bands,
    order_ref, skip_ref, b_hbm, c_hbm, ld_hbm, gain_hbm, x_hbm, gate_hbm, w_hbm,
    out_hbm,
    b_ref, c_ref, ld_ref, gain_ref, sem_in, x_s, gate_s, w_s, p_s, q_s, sem_x, sem_g, sem_w, sem_o,
    col_ref, row_ref, score_ref, bt_s, scale2_s, ecol2_s, dec_s, total_s, prefix_s,
    note_s, gotnote_s, aggnote_s, aggnotes_s, coef_s, before_s, last_s,
    state_s, got_s, agg_s, aggs_s, within_s, carry_s, send_s, ent_s,
    sem_n, sem_a, sem_bn, sem_b, sem_c, pre_s, pregot_s, sem_p,
    entry_s, normed_s, made_s, mine_s, sem,
):
    band, view = lax.axis_index("seq"), lax.axis_index("view")
    count = views * pack
    chips = count // 2
    group, member = band // pack, lax.rem(band, pack)
    me = member * views + view
    heads, tokens = ld_ref.shape
    spans = tokens // GROUP
    width = x_s.shape[1]
    pairs = width // 128
    HALF = GROUP // 2

    load = pltpu.make_async_copy(x_hbm, x_s, sem_x)
    load_gate = pltpu.make_async_copy(gate_hbm, gate_s, sem_g)
    load_w = pltpu.make_async_copy(w_hbm, w_s, sem_w)
    small = [
        pltpu.make_async_copy(source, target, sem_in.at[i])
        for i, (source, target) in enumerate(
            ((ld_hbm, ld_ref), (b_hbm, b_ref), (c_hbm, c_ref), (gain_hbm, gain_ref))
        )
    ]
    for copy in small:
        copy.start()
    load.start()
    load_gate.start()

    barrier = pltpu.get_barrier_semaphore()
    for d in range(1, bands):
        pl.semaphore_signal(
            barrier, inc=1,
            device_id={"seq": lax.rem(band + d, bands), "view": view}, device_id_type=MESH,
        )
    for d in range(1, views):
        for m in range(pack):
            pl.semaphore_signal(
                barrier, inc=1,
                device_id={"seq": group * pack + m, "view": lax.rem(view + d, views)},
                device_id_type=MESH,
            )

    for copy in small:
        copy.wait()
    at_row, at_col = iota((GROUP, GROUP), 0), iota((GROUP, GROUP), 1)
    lower = jnp.where(at_col <= at_row, 1.0, 0.0).astype(BF16)
    upper = jnp.where(at_row <= at_col, 1.0, 0.0).astype(BF16)
    total = jnp.zeros((heads, 1), F32)
    for c in range(spans):
        span = slice(c * GROUP, (c + 1) * GROUP)
        own = ld_ref[:, span] * LOG2E
        padded = jnp.concatenate([own, jnp.zeros((128 - heads, GROUP), F32)], axis=0)
        lines = sum(nn(part, upper) for part in split3(own))
        row_ref[:, span] = lines
        cols = sum(nt(lower, part) for part in split3(padded))
        col_ref[span, :] = cols
        for ref, value in (
            (ecol2_s, jnp.exp2(cols)),
            (scale2_s, jnp.exp2(jnp.minimum(cols[GROUP - 1 : GROUP, :] - cols, 0.0))),
        ):
            hi, lo = split2(value)
            ref[span, 0:128] = hi
            ref[span, 128:256] = lo
        total = total + lines[:, GROUP - 1 : GROUP]
        bt_s[:, span] = b_ref[span, :].astype(F32).T.astype(BF16)
    total_s[...] = jnp.broadcast_to(total, total_s.shape)

    rank = jnp.int32(0)
    for r in range(views):
        rank = rank + jnp.where(order_ref[0, r] == view, r, 0)
    key = (rank + member * views).astype(F32)
    left = iota((1, 128), 1) < 64
    for q in range(count):
        for j in range(batches):
            head = 2 * (j * count + q)
            note_s[q, j : j + 1, :] = jnp.where(
                left, total_s[head : head + 1, :], total_s[head + 1 : head + 2, :]
            )
        note_s[q, batches : batches + 1, :] = jnp.full((1, 128), key, F32)

    def peer(q):
        return {"seq": group * pack + q // views, "view": lax.rem(q, views)}

    def exchange(source, target, sends, receives, q):
        return pltpu.make_async_remote_copy(
            src_ref=source, dst_ref=target, send_sem=sends, recv_sem=receives,
            device_id=peer(q), device_id_type=MESH,
        )

    def note_copy(q, slot):
        return exchange(note_s.at[q], gotnote_s.at[slot], sem_n.at[0, q], sem_n.at[1, slot], q)

    def state_copy(j, q, slot):
        return exchange(
            state_s.at[j, q], got_s.at[j, slot], sem_a.at[j, 0, q], sem_a.at[j, 1, slot], q
        )

    def enter_copy(j, q, slot):
        return exchange(
            send_s.at[j, q], ent_s.at[j, slot], sem_c.at[j, 0, q], sem_c.at[j, 1, slot], q
        )

    mychip = me // 2
    partner = me + 1 - 2 * lax.rem(me, 2)

    def far_chips():
        if chips == 4:
            return [3 - mychip, lax.rem(mychip + 2, 4), mychip + 1 - 2 * lax.rem(mychip, 2)]
        return [lax.rem(mychip + d, chips) for d in range(1, chips)]

    def others():
        return [2 * chip + i for chip in far_chips() for i in range(2)] + [partner]

    def ahead(source, target, sems, k, g):
        return pltpu.make_async_remote_copy(
            src_ref=source, dst_ref=target, send_sem=sems.at[0, k], recv_sem=sems.at[1, k],
            device_id={"seq": g * pack + member, "view": view}, device_id_type=MESH,
        )

    def aggnote_copy(k, g):
        return ahead(aggnote_s, aggnotes_s.at[k], sem_bn, k, g)

    def agg_copy(j, k, g):
        return ahead(agg_s.at[j], aggs_s.at[j, k], sem_b.at[j], k, g)

    even = lax.rem(group, 2) == 0

    def later(run):
        for k in range(groups - 1, 0, -1):
            @pl.when((group + k < groups) & (lax.rem(group + k, 2) == 0))
            def _(k=k):
                run(k, group + k)

    def earlier(run):
        for k in range(groups - 1, 0, -1):
            @pl.when((group - k >= 0) & even)
            def _(k=k):
                run(k, group - k)

    def prefix_copy(j, g):
        return pltpu.make_async_remote_copy(
            src_ref=pre_s.at[j], dst_ref=pregot_s.at[j],
            send_sem=sem_p.at[0, j], recv_sem=sem_p.at[1, j],
            device_id={"seq": g * pack + member, "view": view}, device_id_type=MESH,
        )

    pl.semaphore_wait(barrier, bands - 1 + (views - 1) * pack)
    for q in others():
        note_copy(q, me).start()

    def states(j, chip):
        base = j * count + 2 * chip
        lanes = pl.ds(pl.multiple_of(base * 128, 256), 256)
        pick = spread(2 * base, 256)
        running = jnp.zeros((128, 256), F32)
        for c in range(spans):
            span = slice(c * GROUP, (c + 1) * GROUP)
            scale = nn(scale2_s[span, :], pick)
            made = nn(bt_s[:, span], (x_s[span, lanes].astype(F32) * scale).astype(BF16))
            ends = nn(ecol2_s[(c + 1) * GROUP - 16 : (c + 1) * GROUP, :], pick)
            dec = ends[15:16, :]
            prefix_s[c, :, lanes] = running
            dec_s[c, :, lanes] = jnp.broadcast_to(dec, (8, 256))
            running = dec * running + made if c else made
        for i in range(2):
            state_s[j, 2 * chip + i] = running[:, i * 128 : (i + 1) * 128].astype(BF16)

    load.wait()
    load_w.start()
    for j in range(batches):
        for chip in far_chips():
            states(j, chip)
            for i in range(2):
                state_copy(j, 2 * chip + i, me).start()
        states(j, mychip)
        state_copy(j, partner, me).start()
        got_s[j, me] = state_s[j, me]

    for c in range(spans):
        span = slice(c * GROUP, (c + 1) * GROUP)
        scores = nt(c_ref[span, :], b_ref[span, :])
        score_ref[c] = jnp.where(at_col <= at_row, scores, 0.0)

    first_half = iota((GROUP, 128), 1) < 64

    def inside_span(start, stop):
        @pl.loop(start, stop)
        def _(pair):
            cols = pair_columns(col_ref[...], pair)
            lanes = pl.ds(pl.multiple_of(pair * 128, 128), 128)
            pick = spread(2 * pair, 128)
            for c in range(spans):
                span = slice(c * GROUP, (c + 1) * GROUP)
                x = x_s[span, lanes]
                outs = []
                for j, col in enumerate(cols):
                    line = row_ref[pl.ds(2 * pair + j, 1), span]
                    col = col[span, :]
                    top = jnp.minimum(col[:HALF] - line[:, :HALF], 0.0)
                    top = (jnp.exp2(top) * score_ref[c, :HALF, :HALF]).astype(BF16)
                    low = jnp.minimum(col[HALF:] - line, 0.0)
                    low = (jnp.exp2(low) * score_ref[c, HALF:, :]).astype(BF16)
                    outs.append(jnp.concatenate([nn(top, x[:HALF]), nn(low, x)], axis=0))
                gate = gate_s[span, lanes].astype(F32)
                silu = gate / (1.0 + jnp.exp(-gate))
                q_s[span, lanes] = nn(ecol2_s[span, :], pick) * silu
                made = jnp.where(first_half, outs[0], outs[1]) + jnp.where(
                    first_half, skip_ref[2 * pair], skip_ref[2 * pair + 1]
                ) * x.astype(F32)
                p_s[span, lanes] = made * silu

    cuts = fill_cuts(pairs, batches)
    load_gate.wait()
    inside_span(cuts[0], cuts[1])

    gotnote_s[me] = note_s[me]
    for q in others():
        note_copy(q, q).wait_recv()
    logs = [gotnote_s[b] for b in range(count)]
    keys = [jnp.broadcast_to(log[batches : batches + 1, :], log.shape) for log in logs]
    zero = jnp.zeros_like(logs[0])
    upto, whole = [], zero
    for b in range(count):
        acc = zero
        for o in range(count):
            if o != b:
                acc = acc + jnp.where(keys[o] < keys[b], logs[o], 0.0)
        upto.append(acc + logs[b])
        before_s[b] = jnp.exp2(acc)
        for o in range(count):
            coef_s[b, o] = acc
        whole = whole + logs[b]
    aggnote_s[...] = whole
    later(lambda k, g: aggnote_copy(k, g).start())
    for b in range(count):
        last_s[b] = jnp.exp2(jnp.minimum(whole - upto[b], 0.0))
        for o in range(count):
            if o != b:
                coef_s[b, o] = jnp.where(
                    keys[o] < keys[b], jnp.exp2(jnp.minimum(coef_s[b, o] - upto[o], 0.0)), 0.0
                )

    for j in range(batches):
        for q in others():
            state_copy(j, q, q).wait_recv()
        for i in range(4):
            part = slice(i * 32, (i + 1) * 32)
            acc = jnp.zeros((32, 128), F32)
            for b in range(count):
                acc = acc + last_s[b, j : j + 1, :] * got_s[j, b, part, :].astype(F32)
            agg_s[j, part, :] = acc.astype(BF16)
        later(lambda k, g: agg_copy(j, k, g).start())
        for i in range(4):
            part = slice(i * 32, (i + 1) * 32)
            blocks = [got_s[j, o, part, :].astype(F32) for o in range(count)]
            for b in range(count):
                acc = jnp.zeros((32, 128), F32)
                for o in range(count):
                    if o != b:
                        acc = acc + coef_s[b, o, j : j + 1, :] * blocks[o]
                within_s[j, b, part, :] = acc
        inside_span(cuts[j + 1], cuts[j + 2])

    earlier(lambda k, g: aggnote_copy(k, g).wait_recv())
    for j in range(batches):
        carry_s[...] = jnp.zeros_like(carry_s)

        def gather(k, g):
            agg_copy(j, k, g).wait_recv()
            decay = jnp.exp2(aggnotes_s[k, j : j + 1, :])
            carry_s[...] = decay * carry_s[...] + aggs_s[j, k].astype(F32)

        earlier(gather)

        @pl.when(jnp.logical_not(even))
        def _(j=j):
            prefix_copy(j, group - 1).wait_recv()
            carry_s[...] = pregot_s[j].astype(F32)

        @pl.when(even & (group + 1 < groups))
        def _(j=j):
            decay = jnp.exp2(aggnote_s[j : j + 1, :])
            pre_s[j] = (decay * carry_s[...] + agg_s[j].astype(F32)).astype(BF16)
            prefix_copy(j, group + 1).start()

        def entering(q):
            return (before_s[q, j : j + 1, :] * carry_s[...] + within_s[j, q]).astype(BF16)

        for q in others():
            send_s[j, q] = entering(q)
            enter_copy(j, q, me).start()
        ent_s[j, me] = entering(me)
        inside_span(cuts[batches + j + 1], cuts[batches + j + 2])

    piece = mine_s.shape[1]
    width_out = w_s.shape[1]
    chunk = normed_s.shape[0]
    chunks = tokens // chunk
    half = chunks // 2
    per_chunk = chunk // piece
    turn = lax.rem(band // per_chunk, half)
    mine_half = band // (bands // 2)

    def far_index(i):
        pair = i // 2
        f = (1 - mine_half) * (half // 2 - 1 - pair) + mine_half * pair
        return (1 - mine_half) * half + 2 * f + lax.rem(turn + i, 2)

    def near_index(i):
        return mine_half * half + lax.rem(turn + 1 + i, half)
    same = (iota((256, 256), 0) >> 6) == (iota((256, 256), 1) >> 6)
    block = jnp.where(same, 1.0 / 64.0, 0.0).astype(BF16)
    quads = width // 256

    def send(j):
        return pltpu.make_async_remote_copy(
            src_ref=mine_s.at[j], dst_ref=out_hbm.at[band],
            send_sem=sem.at[0, j], recv_sem=sem.at[1, band],
            device_id={"seq": j, "view": view}, device_id_type=MESH,
        )

    def send_columns(j, cols):
        return pltpu.make_async_remote_copy(
            src_ref=mine_s.at[j, :, cols], dst_ref=out_hbm.at[band, :, cols],
            send_sem=sem.at[0, j], recv_sem=sem.at[1, band],
            device_id={"seq": j, "view": view}, device_id_type=MESH,
        )

    def arrival(i):
        return pltpu.make_async_remote_copy(
            src_ref=mine_s.at[i], dst_ref=out_hbm.at[i],
            send_sem=sem.at[0, i], recv_sem=sem.at[1, i],
            device_id={"seq": i, "view": view}, device_id_type=MESH,
        )

    def entry_of(c, j):
        for q in range(count):
            at = (j * count + q) * 128
            lanes = slice(at, at + 128)
            made = ent_s[j, q].astype(F32)
            entry_s[:, lanes] = (before_of(c, lanes) * made + prefix_s[c, :, lanes]).astype(BF16)

    def before_of(c, lanes):
        made = jnp.ones((1, lanes.stop - lanes.start), F32)
        for o in range(spans - 1):
            made = made * jnp.where(o < c, dec_s[o, 0:1, lanes], 1.0)
        return made

    def gated(rows, quad):
        lanes = slice(quad * 256, (quad + 1) * 256)
        carried = nn(c_ref[rows, :], entry_s[:, lanes])
        g = p_s[rows, lanes] + q_s[rows, lanes] * carried
        high, low = split2(g * g)
        mean = nn(high, block) + nn(low, block)
        normed_s[:, lanes] = (g * lax.rsqrt(mean + EPS) * gain_ref[:, lanes]).astype(BF16)

    def project(index, split=0):
        for n in range(width_out // 256):
            cols = slice(n * 256, (n + 1) * 256)
            made = nn(normed_s[:, split:], w_s[split:, cols])
            if split:
                made = made + made_s[:, cols]
            made = made.astype(BF16)
            for u in range(per_chunk):
                mine_s[index * per_chunk + u, :, cols] = made[u * piece : (u + 1) * piece, :]
            if split and (n % 2 == 1 or n == width_out // 256 - 1):
                for u in range(per_chunk):
                    send_columns(
                        index * per_chunk + u, slice((n - n % 2) * 256, (n + 1) * 256)
                    ).start()
        for u in range(0 if split else per_chunk):
            j = index * per_chunk + u

            @pl.when(j != band)
            def _(j=j):
                send(j).start()

    def rows_of(index):
        return pl.ds(pl.multiple_of(index * chunk, chunk), chunk)

    lead = quads // batches
    split = (batches - 1) * lead * 256
    first = far_index(0)
    c = first * chunk // GROUP
    for j in range(batches):
        for q in others():
            enter_copy(j, q, q).wait_recv()
        entry_of(c, j)
        for quad in range(j * lead, (j + 1) * lead):
            gated(rows_of(first), quad)
        if j == batches - 2:
            load_w.wait()
            for n in range(width_out // 256):
                cols = slice(n * 256, (n + 1) * 256)
                made_s[:, cols] = nn(normed_s[:, :split], w_s[:split, cols])
    if batches == 1:
        load_w.wait()
    project(first, split)

    @pl.loop(1, half)
    def _(i):
        index = far_index(i)
        for quad in range(quads):
            gated(rows_of(index), quad)
        project(index)

    for j in range(batches):
        entry_of(mine_half * half * chunk // GROUP, j)

    @pl.loop(0, half)
    def _(i):
        index = near_index(i)
        for quad in range(quads):
            gated(rows_of(index), quad)
        project(index)

    keep = pltpu.make_async_copy(mine_s.at[band], out_hbm.at[band], sem_o)
    keep.start()
    for q in others():
        note_copy(q, me).wait_send()
        for j in range(batches):
            state_copy(j, q, me).wait_send()
            enter_copy(j, q, me).wait_send()
    later(lambda k, g: aggnote_copy(k, g).wait_send())
    for j in range(batches):
        later(lambda k, g: agg_copy(j, k, g).wait_send())

        @pl.when(even & (group + 1 < groups))
        def _(j=j):
            prefix_copy(j, group + 1).wait_send()

    for d in range(1, bands):
        arrival(lax.rem(band - d + bands, bands)).wait_recv()
    for d in range(1, bands):
        send(lax.rem(band + d, bands)).wait_send()
    keep.wait()


def fill_cuts(pairs, batches):
    shares = [4, 2, 1, 2, 7]
    if batches != 2:
        shares = [1] * (2 * batches + 1)
    return [pairs * sum(shares[:i]) // sum(shares) for i in range(len(shares) + 1)]


def mixer_part(order, skip, b, c, ld, gain, x, gate, w, views, bands):
    heads, tokens = ld.shape
    width, width_out = w.shape
    pack = 2 if bands % 2 == 0 and heads % (4 * views) == 0 else 1
    count = views * pack
    batches = heads // (2 * count)
    groups = bands // pack
    piece = tokens // bands
    spans = tokens // GROUP
    vmem = pl.BlockSpec(memory_space=pltpu.VMEM)
    hbm = pl.BlockSpec(memory_space=pl.ANY)
    smem = pl.BlockSpec(memory_space=pltpu.SMEM)
    dma = pltpu.SemaphoreType.DMA
    sems = lambda *n: dma(n)
    return pl.pallas_call(
        functools.partial(mixer_kernel, views, pack, groups, batches, bands),
        in_specs=[smem] * 2 + [hbm] * 7,
        out_specs=vmem,
        out_shape=VMEM((bands, piece, width_out), BF16),
        scratch_shapes=[
            VMEM(b.shape, BF16),
            VMEM(c.shape, BF16),
            VMEM(ld.shape, F32),
            VMEM(gain.shape, F32),
            sems(4),
            VMEM(x.shape, BF16),
            VMEM(x.shape, BF16),
            VMEM(w.shape, BF16),
            VMEM(x.shape, F32),
            VMEM(x.shape, F32),
            dma, dma, dma, dma,
            VMEM((tokens, 128), F32),
            VMEM((heads, tokens), F32),
            VMEM((spans, GROUP, GROUP), F32),
            VMEM((128, tokens), BF16),
            VMEM((tokens, 256), BF16),
            VMEM((tokens, 256), BF16),
            VMEM((spans, 8, width), F32),
            VMEM((heads, 128), F32),
            VMEM((spans, 128, width), F32),
            VMEM((count, 8, 128), F32),
            VMEM((count, 8, 128), F32),
            VMEM((8, 128), F32),
            VMEM((groups, 8, 128), F32),
            VMEM((count, count, 8, 128), F32),
            VMEM((count, 8, 128), F32),
            VMEM((count, 8, 128), F32),
            VMEM((batches, count, 128, 128), BF16),
            VMEM((batches, count, 128, 128), BF16),
            VMEM((batches, 128, 128), BF16),
            VMEM((batches, groups, 128, 128), BF16),
            VMEM((batches, count, 128, 128), F32),
            VMEM((128, 128), F32),
            VMEM((batches, count, 128, 128), BF16),
            VMEM((batches, count, 128, 128), BF16),
            sems(2, count), sems(batches, 2, count), sems(2, groups),
            sems(batches, 2, groups), sems(batches, 2, count),
            VMEM((batches, 128, 128), BF16),
            VMEM((batches, 128, 128), BF16),
            sems(2, batches),
            VMEM((128, width), BF16),
            VMEM((max(piece, TILE // 2), width), BF16),
            VMEM((max(piece, TILE // 2), width_out), F32),
            VMEM((bands, piece, width_out), BF16),
            sems(2, bands),
        ],
        compiler_params=pltpu.CompilerParams(
            collective_id=0, has_side_effects=True, vmem_limit_bytes=VMEM_LIMIT
        ),
        name="mixer_part",
    )(order, skip, b, c, ld, gain, x, gate, w)


def tile_kernel(order_ref, in_ref, out_hbm, sems):
    tiles = order_ref.shape[0]
    per = in_ref.shape[0] // tiles

    def put(k):
        return pltpu.make_async_copy(
            in_ref.at[pl.ds(order_ref[k] * per, per)],
            out_hbm.at[k * per : (k + 1) * per],
            sems.at[k],
        )

    for k in range(tiles):
        put(k).start()
    for k in range(tiles):
        put(k).wait()


def tile_part(order, pieces):
    bands, piece, width = pieces.shape
    tiles = order.shape[0]
    return pl.pallas_call(
        tile_kernel,
        in_specs=[
            pl.BlockSpec(memory_space=pltpu.SMEM),
            pl.BlockSpec(memory_space=pl.ANY),
        ],
        out_specs=pl.BlockSpec(memory_space=pl.ANY),
        out_shape=jax.ShapeDtypeStruct(pieces.shape, BF16),
        scratch_shapes=[pltpu.SemaphoreType.DMA((tiles,))],
        compiler_params=pltpu.CompilerParams(vmem_limit_bytes=VMEM_LIMIT // 16),
        name="tile_part",
    )(order, pieces)


def shards(
    ssd_input, gate_input, b_matrix, c_matrix, log_decay,
    d_skip, norm_gain, out_weight, view_order, tile_order,
):
    views, bands = lax.axis_size("view"), lax.axis_size("seq")
    x, gate = ssd_input[0, 0], gate_input[0, 0]
    b, c, ld = b_matrix[0, 0], c_matrix[0, 0], log_decay[0, 0]
    tokens, width = x.shape
    pieces = mixer_part(
        view_order, d_skip, b, c, ld, norm_gain[None, :], x, gate, out_weight, views, bands
    )
    out = tile_part(tile_order[0], pieces)
    return out.reshape(1, 1, tokens, out_weight.shape[1])


def solution(mesh):
    whole = P("seq", "view", None, None)
    in_specs = (whole,) * 5 + (P(), P(), P(), P("seq", None), P("seq", None))
    return jax.shard_map(
        shards, mesh=mesh, in_specs=in_specs, out_specs=whole, check_vma=False
    )
```
